32 devices in a mesh: face: 2 (over y), tx: 4 (over z), ty: 4 (over x, core).
Axes of the slice: x: 2, y: 2, z: 4, core: 2. Of those that a mesh axis runs over, the one named last changes fastest.
Arguments:
- probes: float32 [2, 4, 2, 6, 32, 32], P(None, None, 'face', None, 'tx', 'ty'), may hold values from -6 to 6
- background_wind: float32 [2, 2, 6, 32, 32], P(None, 'face', None, 'tx', 'ty'), may hold values from -6 to 6
- layer_mass: float32 [2, 6, 32, 32], P('face', None, 'tx', 'ty'), may hold values from 0.5 to 2
- trajectory_heat_factor: float32 [2, 6, 32, 32], P('face', None, 'tx', 'ty'), may hold values from 0.3 to 3
- spread: float32 [4, 2, 6, 32, 32], P(None, 'face', None, 'tx', 'ty'), may hold values from 0.5 to 2
- inverse_misfit_variance: float32 [4, 2, 6, 32, 32], P(None, 'face', None, 'tx', 'ty'), may hold values from 0.25 to 4
- face_links: int32 [6, 4, 7], replicated, may hold values from -1 to 5, as said below
Outputs:
- applied: float32 [2, 4, 2, 6, 32, 32], P(None, None, 'face', None, 'tx', 'ty')
The draws below stay inside these ranges and needn't reach their ends.
Inputs may be any that keep to these rules, and one draw needn't show every extreme that they name: `face_links`: the table describes the six panels of a cube, each with a right-handed frame: for panel f and edge e, the panel across it, the edge of that panel which touches f, whether the index along the shared edge runs the other way, and the matrix of entries -1, 0, 1 that carries vector components from that panel's frame into the frame of f.
All inputs are finite; a program needn't handle non-finite values.
Results may differ from the reference program's by a relative error of at most 0.00002.
Values sent between devices are 32-bit elements; how exact they have to be, the bound alone decides.
A program may use at most 64 MiB of HBM per device.

```python
import math
import jax
import jax.numpy as jnp

PROBES = 2
LEV = 2
SIDE = 32


def draw_face_links(key, part):
    centre = jnp.array([[1, 0, 0], [-1, 0, 0], [0, 1, 0], [0, -1, 0], [0, 0, 1], [0, 0, -1]], jnp.int32)
    across = jnp.array([[0, 1, 0], [0, 0, 1], [0, 0, 1], [1, 0, 0], [1, 0, 0], [0, 1, 0]], jnp.int32)
    upward = jnp.array([[0, 0, 1], [0, 1, 0], [1, 0, 0], [0, 0, 1], [0, 1, 0], [1, 0, 0]], jnp.int32)
    order = jax.random.permutation(jax.random.fold_in(key, 11), 6)
    quarter = jax.random.randint(jax.random.fold_in(key, 12), (6,), 0, 4)
    centre = centre[order]
    across = across[order]
    upward = upward[order]
    turned = quarter[:, None]
    new_across = jnp.where(turned == 0, across, jnp.where(turned == 1, upward, jnp.where(turned == 2, -across, -upward)))
    new_upward = jnp.where(turned == 0, upward, jnp.where(turned == 1, -across, jnp.where(turned == 2, -upward, across)))
    across = new_across
    upward = new_upward
    outward = jnp.stack([-across, across, -upward, upward], axis=1)
    along_edge = jnp.stack([upward, upward, across, across], axis=1)
    hits = jnp.all(outward[:, :, None, :] == centre[None, None, :, :], axis=-1)
    neighbour = jnp.sum(hits.astype(jnp.int32) * jnp.arange(6, dtype=jnp.int32), axis=-1)
    far_out = outward[neighbour]
    back_hits = jnp.all(far_out == centre[:, None, None, :], axis=-1).astype(jnp.int32)
    far_edge = jnp.sum(back_hits * jnp.arange(4, dtype=jnp.int32), axis=-1)
    far_along = jnp.sum(back_hits[..., None] * along_edge[neighbour], axis=2)
    reverse = (jnp.sum(along_edge * far_along, axis=-1) < 0).astype(jnp.int32)
    near_centre = centre[:, None, :]
    folding = near_centre + outward

    def carried(vectors):
        return vectors - jnp.sum(vectors * near_centre, axis=-1, keepdims=True) * folding

    def projected(vectors, basis):
        return jnp.sum(vectors * basis, axis=-1)
    far_across = carried(across[neighbour])
    far_upward = carried(upward[neighbour])
    near_across = across[:, None, :]
    near_upward = upward[:, None, :]
    table = jnp.stack([neighbour, far_edge, reverse, projected(far_across, near_across), projected(far_upward, near_across), projected(far_across, near_upward), projected(far_upward, near_upward)], axis=-1)
    return table.astype(jnp.int32)


def steps_of(key, extent, split, smallest, top_value):
    level = 1.0
    for position, blocks in split:
        steps = jax.random.uniform(jax.random.fold_in(jax.random.fold_in(key, 6), position), (blocks,), jnp.float32, smallest / len(split), top_value / len(split))
        level = level * jnp.repeat(jnp.exp(steps), extent[position] // blocks).reshape((-1,) + (1,) * (len(extent) - 1 - position))
    return level


def gaussian(stream_key, shape, scale, reach, cuts=(), held_as=jnp.bfloat16):
    values = jax.random.normal(stream_key, shape, jnp.float32) * scale
    if len(cuts) > 0:
        values = steps_of(stream_key, shape, cuts, -0.22, 0.18) * values
    return jnp.clip(values, min=-reach, max=reach).astype(held_as)


def setup_inputs(seed: int = 0) -> dict:
    splits = jax.random.split(jax.random.key(seed), 8)
    probes = gaussian(splits[0], (PROBES, 4, LEV, 6, SIDE, SIDE), 1.0, 6.0, ((2, 2), (4, 4), (5, 4)), jnp.float32)
    background_wind = gaussian(splits[1], (2, LEV, 6, SIDE, SIDE), 1.0, 6.0, ((1, 2), (3, 4), (4, 4)), jnp.float32)
    layer_mass = jnp.clip(jnp.exp(math.log(2.0) - 1.3862944 * jax.random.uniform(splits[2], (LEV, 6, SIDE, SIDE), jnp.float32) ** steps_of(splits[2], (LEV, 6, SIDE, SIDE), ((0, 2), (2, 4), (3, 4)), -0.2, 0.2)), 0.5, 2.0)
    trajectory_heat_factor = jnp.clip(jnp.exp(math.log(3.0) - 2.3025851 * jax.random.uniform(splits[3], (LEV, 6, SIDE, SIDE), jnp.float32) ** steps_of(splits[3], (LEV, 6, SIDE, SIDE), ((0, 2), (2, 4), (3, 4)), -0.2, 0.2)), 0.3, 3.0)
    spread = jnp.clip(jnp.exp(math.log(2.0) - 1.3862944 * jax.random.uniform(splits[4], (4, LEV, 6, SIDE, SIDE), jnp.float32) ** steps_of(splits[4], (4, LEV, 6, SIDE, SIDE), ((1, 2), (3, 4), (4, 4)), -0.2, 0.2)), 0.5, 2.0)
    inverse_misfit_variance = jnp.clip(jnp.exp(math.log(4.0) - 2.7725887 * jax.random.uniform(splits[5], (4, LEV, 6, SIDE, SIDE), jnp.float32) ** steps_of(splits[5], (4, LEV, 6, SIDE, SIDE), ((1, 2), (3, 4), (4, 4)), -0.2, 0.2)), 0.25, 4.0)
    face_links = draw_face_links(jax.random.fold_in(splits[7], 71), 0)
    return dict(probes=probes, background_wind=background_wind, layer_mass=layer_mass, trajectory_heat_factor=trajectory_heat_factor, spread=spread, inverse_misfit_variance=inverse_misfit_variance, face_links=face_links)


time_increment = 0.3
forward_layout = (('vector', 0), ('vector', 2), ('scalar', 4), ('scalar', 5))

def carry_pair(leading, trailing, entries):
    return (entries[0] * leading + entries[1] * trailing, entries[2] * leading + entries[3] * trailing)

def rotate_edge(edge_strip, matrix_codes, layout):
    matrix = matrix_codes.astype(edge_strip.dtype)
    entries = [matrix[:, column].reshape(1, 1, 6, 1) for column in range(4)]
    channels = [edge_strip[number] for number in range(edge_strip.shape[0])]
    for species, offset in layout:
        if species == 'vector':
            channels[offset], channels[offset + 1] = carry_pair(channels[offset], channels[offset + 1], entries)
        elif species == 'tensor':
            channels[offset], channels[offset + 1] = carry_pair(channels[offset], channels[offset + 1], entries)
            channels[offset + 2], channels[offset + 3] = carry_pair(channels[offset + 2], channels[offset + 3], entries)
            channels[offset], channels[offset + 2] = carry_pair(channels[offset], channels[offset + 2], entries)
            channels[offset + 1], channels[offset + 3] = carry_pair(channels[offset + 1], channels[offset + 3], entries)
    return jnp.stack(channels)

def orient(edge_rows, face_links, side, layout):
    source_face = face_links[:, side, 0]
    source_edge = face_links[:, side, 1]
    chosen = edge_rows[:, :, :, source_face, source_edge, :]
    flipped = (face_links[:, side, 2] == 1).reshape(1, 1, 1, 6, 1)
    chosen = jnp.where(flipped, chosen[..., ::-1], chosen)
    return rotate_edge(chosen, face_links[:, side, 3:7], layout)

def extend(fields, face_links, layout):
    edge_rows = jnp.stack([fields[..., 0, :], fields[..., -1, :], fields[..., :, 0], fields[..., :, -1]], axis=4)
    padded = jnp.pad(fields, ((0, 0), (0, 0), (0, 0), (0, 0), (1, 1), (1, 1)))
    padded = padded.at[..., 0, 1:-1].set(orient(edge_rows, face_links, 0, layout))
    padded = padded.at[..., -1, 1:-1].set(orient(edge_rows, face_links, 1, layout))
    padded = padded.at[..., 1:-1, 0].set(orient(edge_rows, face_links, 2, layout))
    padded = padded.at[..., 1:-1, -1].set(orient(edge_rows, face_links, 3, layout))
    return padded

def slopes(padded):
    east_slope_derivative = 0.5 * (padded[..., 2:, 1:-1] - padded[..., :-2, 1:-1])
    north_slope_derivative = 0.5 * (padded[..., 1:-1, 2:] - padded[..., 1:-1, :-2])
    return (east_slope_derivative, north_slope_derivative)

def tangent(normalised_state_array, background_wind, layer_mass, trajectory_heat_factor, face_links):
    west_east_wind_part, south_north_wind_speed, sheet_depth_state, sheet_warmth_state = (normalised_state_array[:, 0], normalised_state_array[:, 1], normalised_state_array[:, 2], normalised_state_array[:, 3])
    east_wind_speed, north_wind_speed = (background_wind[0], background_wind[1])
    ground_barometric_load = jnp.cumsum(sheet_depth_state, axis=1)
    gravity_potential_level = sheet_warmth_state + trajectory_heat_factor * ground_barometric_load
    east_mass_transport = east_wind_speed * sheet_depth_state + layer_mass * west_east_wind_part
    north_mass_transport = north_wind_speed * sheet_depth_state + layer_mass * south_north_wind_speed
    joined_state_arrays = jnp.stack([west_east_wind_part, south_north_wind_speed, east_mass_transport, north_mass_transport, sheet_warmth_state, gravity_potential_level])
    east_slope_derivative, north_slope_derivative = slopes(extend(joined_state_arrays, face_links, forward_layout))
    west_east_wind_after = west_east_wind_part - time_increment * (east_slope_derivative[5] + east_wind_speed * east_slope_derivative[0] + north_wind_speed * north_slope_derivative[0])
    south_north_wind_after = south_north_wind_speed - time_increment * (north_slope_derivative[5] + east_wind_speed * east_slope_derivative[1] + north_wind_speed * north_slope_derivative[1])
    depth_after_update = sheet_depth_state - time_increment * (east_slope_derivative[2] + north_slope_derivative[3])
    warmth_after_update = sheet_warmth_state - time_increment * (east_wind_speed * east_slope_derivative[4] + north_wind_speed * north_slope_derivative[4])
    return jnp.stack([west_east_wind_after, south_north_wind_after, depth_after_update, warmth_after_update], axis=1)

def reference(probes, background_wind, layer_mass, trajectory_heat_factor, spread, inverse_misfit_variance, face_links):
    normalised_state_array = spread[None] * probes

    def linear_step(perturbed):
        return tangent(perturbed, background_wind, layer_mass, trajectory_heat_factor, face_links)
    model_image, pullback = jax.vjp(linear_step, normalised_state_array)
    adjoint_out, = pullback(inverse_misfit_variance[None] * model_image)
    return probes + spread[None] * adjoint_out
```

```python
import functools

import jax
import jax.numpy as jnp
from jax import lax
from jax.experimental import pallas as pl
from jax.experimental.pallas import tpu as pltpu
from jax.sharding import PartitionSpec as P

MESH = pl.DeviceIdType.MESH
SUBLANES = 8
LANES = 128

time_increment = 0.3
forward_layout = (("vector", 0), ("vector", 2), ("scalar", 4), ("scalar", 5))
adjoint_layout = (("tensor", 0), ("vector", 4), ("scalar", 6), ("vector", 7))


def padded_2(array, sides, width):
    for axis, dim in sides:
        devices, length = (lax.axis_size(axis), array.shape[dim])
        up = [(i, (i + 1) % devices) for i in range(devices - 1)]
        down = [(j, i) for i, j in up]
        last = lax.slice_in_dim(array, length - width, length, axis=dim)
        leading = lax.slice_in_dim(array, 0, width, axis=dim)
        before = lax.ppermute(last, axis, up)
        after = lax.ppermute(leading, axis, down)
        array = jnp.concatenate([before, array, after], axis=dim)
    return array


def carried_in(value, axis, join, neutral, backward):
    count, mine = (lax.axis_size(axis), lax.axis_index(axis))
    pieces = lax.all_gather(value, axis)
    if backward:
        pieces = pieces[::-1]
        mine = count - 1 - mine
    total = jnp.full_like(value, 0) + jnp.asarray(neutral, value.dtype)

    def hop(position, total):
        longer = join(total, pieces[position])
        return jnp.where(position < mine, longer, total)

    return lax.fori_loop(0, count - 1, hop, total)


def carry_pair(leading, trailing, entries):
    return (
        entries[0] * leading + entries[1] * trailing,
        entries[2] * leading + entries[3] * trailing,
    )


def rotate_edge(edge_strip, matrix_codes, layout):
    matrix = matrix_codes.astype(edge_strip.dtype)
    entries = [matrix[:, column].reshape(1, 1, 6, 1) for column in range(4)]
    channels = [edge_strip[number] for number in range(edge_strip.shape[0])]
    for species, offset in layout:
        if species == "vector":
            channels[offset], channels[offset + 1] = carry_pair(
                channels[offset], channels[offset + 1], entries
            )
        elif species == "tensor":
            channels[offset], channels[offset + 1] = carry_pair(
                channels[offset], channels[offset + 1], entries
            )
            channels[offset + 2], channels[offset + 3] = carry_pair(
                channels[offset + 2], channels[offset + 3], entries
            )
            channels[offset], channels[offset + 2] = carry_pair(
                channels[offset], channels[offset + 2], entries
            )
            channels[offset + 1], channels[offset + 3] = carry_pair(
                channels[offset + 1], channels[offset + 3], entries
            )
    return jnp.stack(channels)


def orient(edge_rows, face_links, side, layout):
    source_face = face_links[:, side, 0]
    source_edge = face_links[:, side, 1]
    chosen = edge_rows[:, :, :, source_face, source_edge, :]
    flipped = (face_links[:, side, 2] == 1).reshape(1, 1, 1, 6, 1)
    chosen = jnp.where(flipped, chosen[..., ::-1], chosen)
    return rotate_edge(chosen, face_links[:, side, 3:7], layout)


def face_rows(fields):
    tile_row = lax.axis_index("tx")
    tile_column = lax.axis_index("ty")
    low_rows = jnp.where(tile_row == 0, fields[..., 0, :], 0.0)
    high_rows = jnp.where(tile_row == lax.axis_size("tx") - 1, fields[..., -1, :], 0.0)
    low_columns = jnp.where(tile_column == 0, fields[..., :, 0], 0.0)
    high_columns = jnp.where(tile_column == lax.axis_size("ty") - 1, fields[..., :, -1], 0.0)
    row_pair = jnp.stack([low_rows, high_rows], axis=4)
    column_pair = jnp.stack([low_columns, high_columns], axis=4)
    row_full = lax.psum(lax.all_gather(row_pair, "ty", axis=5, tiled=True), "tx")
    column_full = lax.psum(lax.all_gather(column_pair, "tx", axis=5, tiled=True), "ty")
    return jnp.concatenate([row_full, column_full], axis=4)


def extended_slopes(fields, face_links, layout):
    row_cells = fields.shape[4]
    column_cells = fields.shape[5]
    tile_row = lax.axis_index("tx")
    tile_column = lax.axis_index("ty")
    padded = padded_2(fields, (("tx", 4), ("ty", 5)), 1)
    edge_rows = face_rows(fields)
    western = lax.dynamic_slice_in_dim(
        orient(edge_rows, face_links, 0, layout), tile_column * column_cells, column_cells, 4
    )
    eastern = lax.dynamic_slice_in_dim(
        orient(edge_rows, face_links, 1, layout), tile_column * column_cells, column_cells, 4
    )
    southern = lax.dynamic_slice_in_dim(
        orient(edge_rows, face_links, 2, layout), tile_row * row_cells, row_cells, 4
    )
    northern = lax.dynamic_slice_in_dim(
        orient(edge_rows, face_links, 3, layout), tile_row * row_cells, row_cells, 4
    )
    row_number = lax.broadcasted_iota(jnp.int32, (row_cells, column_cells), 0)
    column_number = lax.broadcasted_iota(jnp.int32, (row_cells, column_cells), 1)
    first_row = (row_number == 0) & (tile_row == 0)
    last_row = (row_number == row_cells - 1) & (tile_row == lax.axis_size("tx") - 1)
    first_column = (column_number == 0) & (tile_column == 0)
    last_column = (column_number == column_cells - 1) & (tile_column == lax.axis_size("ty") - 1)
    east_slope_derivative = 0.5 * (padded[..., 2:, 1:-1] - padded[..., :-2, 1:-1])
    east_slope_derivative = (
        east_slope_derivative
        + jnp.where(last_row, 0.5 * eastern[..., None, :], 0.0)
        - jnp.where(first_row, 0.5 * western[..., None, :], 0.0)
    )
    north_slope_derivative = 0.5 * (padded[..., 1:-1, 2:] - padded[..., 1:-1, :-2])
    north_slope_derivative = (
        north_slope_derivative
        + jnp.where(last_column, 0.5 * northern[..., :, None], 0.0)
        - jnp.where(first_column, 0.5 * southern[..., :, None], 0.0)
    )
    return (east_slope_derivative, north_slope_derivative)


def pressure_of(sheet_depth_state):
    within = jnp.cumsum(sheet_depth_state, axis=1)
    totals_here = within[:, -1]
    underneath = carried_in(totals_here, "face", jnp.add, jnp.zeros_like(totals_here), False)
    return within + underneath[:, None]


def load_of(sensitivity):
    within = jnp.flip(jnp.cumsum(jnp.flip(sensitivity, 1), axis=1), 1)
    totals_here = within[:, 0]
    overhead = carried_in(totals_here, "face", jnp.add, jnp.zeros_like(totals_here), True)
    return within + overhead[:, None]


def body(
    probes,
    background_wind,
    layer_mass,
    trajectory_heat_factor,
    spread,
    inverse_misfit_variance,
    face_links,
):
    normalised_state_array = spread[None] * probes
    west_east_wind_part, south_north_wind_speed, sheet_depth_state, sheet_warmth_state = (
        normalised_state_array[:, 0],
        normalised_state_array[:, 1],
        normalised_state_array[:, 2],
        normalised_state_array[:, 3],
    )
    east_wind_speed, north_wind_speed = (background_wind[0], background_wind[1])
    ground_barometric_load = pressure_of(sheet_depth_state)
    gravity_potential_level = sheet_warmth_state + trajectory_heat_factor * ground_barometric_load
    east_mass_transport = east_wind_speed * sheet_depth_state + layer_mass * west_east_wind_part
    north_mass_transport = (
        north_wind_speed * sheet_depth_state + layer_mass * south_north_wind_speed
    )
    joined_state_arrays = jnp.stack(
        [
            west_east_wind_part,
            south_north_wind_speed,
            east_mass_transport,
            north_mass_transport,
            sheet_warmth_state,
            gravity_potential_level,
        ]
    )
    east_slope_derivative, north_slope_derivative = extended_slopes(
        joined_state_arrays, face_links, forward_layout
    )
    west_east_wind_after = west_east_wind_part - time_increment * (
        east_slope_derivative[5]
        + east_wind_speed * east_slope_derivative[0]
        + north_wind_speed * north_slope_derivative[0]
    )
    south_north_wind_after = south_north_wind_speed - time_increment * (
        north_slope_derivative[5]
        + east_wind_speed * east_slope_derivative[1]
        + north_wind_speed * north_slope_derivative[1]
    )
    depth_after_update = sheet_depth_state - time_increment * (
        east_slope_derivative[2] + north_slope_derivative[3]
    )
    warmth_after_update = sheet_warmth_state - time_increment * (
        east_wind_speed * east_slope_derivative[4] + north_wind_speed * north_slope_derivative[4]
    )
    zonal_cost = inverse_misfit_variance[0] * west_east_wind_after
    meridional_cost = inverse_misfit_variance[1] * south_north_wind_after
    thickness_cost = inverse_misfit_variance[2] * depth_after_update
    heat_misfit_penalty = inverse_misfit_variance[3] * warmth_after_update
    sensitive = jnp.stack(
        [
            east_wind_speed * zonal_cost,
            east_wind_speed * meridional_cost,
            north_wind_speed * zonal_cost,
            north_wind_speed * meridional_cost,
            zonal_cost,
            meridional_cost,
            thickness_cost,
            east_wind_speed * heat_misfit_penalty,
            north_wind_speed * heat_misfit_penalty,
        ]
    )
    east_slope_derivative, north_slope_derivative = extended_slopes(
        sensitive, face_links, adjoint_layout
    )
    geo_back = time_increment * (east_slope_derivative[4] + north_slope_derivative[5])
    flux_east_back = time_increment * east_slope_derivative[6]
    flux_north_back = time_increment * north_slope_derivative[6]
    zonal_back = (
        zonal_cost
        + time_increment * (east_slope_derivative[0] + north_slope_derivative[2])
        + layer_mass * flux_east_back
    )
    meridional_back = (
        meridional_cost
        + time_increment * (east_slope_derivative[1] + north_slope_derivative[3])
        + layer_mass * flux_north_back
    )
    warmth_back = (
        heat_misfit_penalty
        + time_increment * (east_slope_derivative[7] + north_slope_derivative[8])
        + geo_back
    )
    thickness_back = (
        thickness_cost
        + east_wind_speed * flux_east_back
        + north_wind_speed * flux_north_back
        + load_of(trajectory_heat_factor * geo_back)
    )
    adjoint_out = jnp.stack([zonal_back, meridional_back, thickness_back, warmth_back], axis=1)
    return probes + spread[None] * adjoint_out


def rolled(tile, shift, axis):
    return pltpu.roll(tile, shift % tile.shape[axis], axis)


def block_transposed(tile, sub, inner):
    step = SUBLANES // 2
    while step:
        ahead = rolled(rolled(tile, -step, 0), step, 1)
        behind = rolled(rolled(tile, step, 0), -step, 1)
        low_row = (sub & step) == 0
        low_lane = (inner & step) == 0
        tile = jnp.where(low_row == low_lane, tile, jnp.where(low_row, ahead, behind))
        step //= 2
    return tile


def block_reversed(tile, inner):
    step = SUBLANES // 2
    while step:
        tile = jnp.where(
            (inner & step) == 0, rolled(tile, -step, 1), rolled(tile, step, 1)
        )
        step //= 2
    return tile


def tile_kernel(
    count,
    faces,
    probes_ref,
    wind_ref,
    mass_ref,
    heat_ref,
    spread_ref,
    variance_ref,
    links_ref,
    out_ref,
    strips_f,
    strips_a,
    halo_f,
    halo_a,
    slots_f,
    slots_a,
    below_ref,
    above_ref,
    column_f,
    column_a,
    send_f,
    send_a,
    recv_halo_f,
    recv_halo_a,
    recv_slot_f,
    recv_slot_a,
    send_below,
    send_above,
    recv_below,
    recv_above,
):
    level = lax.axis_index("face")
    row = lax.axis_index("tx")
    column = lax.axis_index("ty")
    probe_count = probes_ref.shape[0]
    panels = probes_ref.shape[3]
    last = count - 1
    at = [row == 0, row == last, column == 0, column == last]
    on_row = at[0] | at[1]
    on_column = at[2] | at[3]
    corner = on_row & on_column
    middle = (on_row | on_column) & ~corner
    row_edge = jnp.where(at[0], 0, 1)
    column_edge = jnp.where(at[2], 2, 3)
    half = count // 2
    row_part = jnp.where(column < half, 0, 1)
    column_part = jnp.where(row < half, 0, 1)
    row_slot = row_edge * 2 + row_part
    column_slot = column_edge * 2 + column_part
    own_edge = jnp.where(on_row, row_edge, column_edge)
    own_slot = jnp.where(on_row, row_slot, column_slot)
    along = jnp.where(on_row, column, row)
    near = jnp.where(along < half, along, last - along)

    def slot_place(edge, part):
        segment = near if part == 0 else last - near
        return [(0, segment), (last, segment), (segment, 0), (segment, last)][edge]

    beside = [(row - 1, column), (row + 1, column), (row, column - 1), (row, column + 1)]
    corners = [(0, 0), (0, last), (last, 0), (last, last)]

    barrier = pltpu.get_barrier_semaphore()

    def greet(place):
        pl.semaphore_signal(
            barrier,
            inc=1,
            device_id={"tx": place[0], "ty": place[1]},
            device_id_type=MESH,
        )

    for d in range(4):
        @pl.when(~at[d])
        def _():
            greet(beside[d])

    @pl.when(middle)
    def _():
        for slot in range(8):
            @pl.when(own_slot != slot)
            def _():
                greet(slot_place(slot // 2, slot % 2))

    @pl.when(corner)
    def _():
        for place in corners:
            @pl.when((row != place[0]) | (column != place[1]))
            def _():
                greet(place)

    for other in range(faces):
        @pl.when(level != other)
        def _():
            pl.semaphore_signal(
                barrier, inc=1, device_id={"face": other}, device_id_type=MESH
            )

    expected = faces - 1 + jnp.where(middle, 7, 0) + jnp.where(corner, 3, 0)
    for d in range(4):
        expected = expected + jnp.where(at[d], 0, 1)

    sub = lax.broadcasted_iota(jnp.int32, (SUBLANES, LANES), 0)
    lane = lax.broadcasted_iota(jnp.int32, (SUBLANES, LANES), 1)
    inner = lane % SUBLANES
    panel_of = (lane // SUBLANES) % panels

    def packed(tiles):
        width = LANES - SUBLANES * len(tiles)
        return jnp.concatenate(tiles + [jnp.zeros((SUBLANES, width), jnp.float32)], axis=1)

    def per_panel(load):
        return packed([load(f) for f in range(panels)] * probe_count)

    def per_probe(component):
        return packed(
            [
                probes_ref[p, component, 0, f]
                for p in range(probe_count)
                for f in range(panels)
            ]
        )

    def level_copy(other, source, target, send, recv):
        return pltpu.make_async_remote_copy(
            src_ref=source,
            dst_ref=target,
            send_sem=send,
            recv_sem=recv,
            device_id={"face": other},
            device_id_type=MESH,
        )

    def below_copy(other, slot):
        return level_copy(
            other, column_f, below_ref.at[slot], send_below.at[other], recv_below.at[slot]
        )

    def above_copy(other, slot):
        return level_copy(
            other, column_a, above_ref.at[slot], send_above.at[other], recv_above.at[slot]
        )

    probe_h = per_probe(2)
    spread_h = per_panel(lambda f: spread_ref[2, 0, f])
    h = spread_h * probe_h
    column_f[...] = h
    pl.semaphore_wait(barrier, expected)
    for other in range(1, faces):
        @pl.when(level < other)
        def _():
            below_copy(other, level).start()

    probe_z, probe_m, probe_t = per_probe(0), per_probe(1), per_probe(3)
    spread_z, spread_m, spread_t = [
        per_panel(lambda f, c=c: spread_ref[c, 0, f]) for c in (0, 1, 3)
    ]
    u, v = [per_panel(lambda f, c=c: wind_ref[c, 0, f]) for c in range(2)]
    mass = per_panel(lambda f: mass_ref[0, f])
    heat = per_panel(lambda f: heat_ref[0, f])
    z, m, t = spread_z * probe_z, spread_m * probe_m, spread_t * probe_t
    fx = u * h + mass * z
    fy = v * h + mass * m

    def write_strips(strips, x_fields, y_fields):
        low = jnp.zeros((SUBLANES, LANES), jnp.float32)
        high = low
        for c, field in enumerate(x_fields):
            low = jnp.where(sub == c, field[0:1, :], low)
            high = jnp.where(sub == c, field[SUBLANES - 1 : SUBLANES, :], high)
        strips[0] = low
        strips[1] = high
        low = jnp.zeros((SUBLANES, LANES), jnp.float32)
        high = low
        for c, field in enumerate(y_fields):
            low = jnp.where(inner == c, rolled(field, c, 1), low)
            high = jnp.where(inner == c, rolled(field, c - (SUBLANES - 1), 1), high)
        strips[2] = block_transposed(low, sub, inner)
        strips[3] = block_transposed(high, sub, inner)

    def strip_copy(source, target, send, recv, place):
        return pltpu.make_async_remote_copy(
            src_ref=source,
            dst_ref=target,
            send_sem=send,
            recv_sem=recv,
            device_id={"tx": place[0], "ty": place[1]},
            device_id_type=MESH,
        )

    def each_send(strips, halo, slots, send, recv_halo, recv_slot, act):
        @pl.when(middle)
        def _():
            for slot in range(8):
                @pl.when(own_slot != slot)
                def _():
                    act(
                        strip_copy(
                            strips.at[own_edge],
                            slots.at[own_slot],
                            send.at[4 + slot],
                            recv_slot.at[own_slot],
                            slot_place(slot // 2, slot % 2),
                        )
                    )

        @pl.when(corner)
        def _():
            for number, place in enumerate(corners):
                @pl.when((row != place[0]) | (column != place[1]))
                def _():
                    for kind, (edge, slot) in enumerate(
                        ((row_edge, row_slot), (column_edge, column_slot))
                    ):
                        act(
                            strip_copy(
                                strips.at[edge],
                                slots.at[slot],
                                send.at[4 + number * 2 + kind],
                                recv_slot.at[slot],
                                place,
                            )
                        )

        for d in range(4):
            @pl.when(~at[d])
            def _():
                act(
                    strip_copy(
                        strips.at[d],
                        halo.at[d ^ 1],
                        send.at[d],
                        recv_halo.at[d ^ 1],
                        beside[d],
                    )
                )

    def ghost_across(slots, edge, part, is_row, is_adjoint):
        strip = jnp.zeros((SUBLANES, LANES), jnp.float32)
        reverse = jnp.zeros((SUBLANES, LANES), jnp.int32)
        entries = [strip] * 4
        for f in range(panels):
            source = links_ref[f, edge, 0]
            flip = links_ref[f, edge, 2]
            slot = links_ref[f, edge, 1] * 2 + jnp.where(flip == 1, 1 - part, part)
            shift = (SUBLANES * (f - source) + LANES) % LANES
            here = panel_of == f
            strip = jnp.where(here, pltpu.roll(slots[slot], shift, 1), strip)
            reverse = jnp.where(here, flip, reverse)
            entries = [
                jnp.where(here, links_ref[f, edge, 3 + i].astype(jnp.float32), entries[i])
                for i in range(4)
            ]
        strip = jnp.where(reverse == 1, block_reversed(strip, inner), strip)
        m0, m1, m2, m3 = entries
        normal = m0 + m1 if is_row else m2 + m3
        first = m0 * strip + m1 * rolled(strip, -1, 0)
        second = m3 * strip + m2 * rolled(strip, 1, 0)
        if is_adjoint:
            vectors = jnp.where(sub == 0, first, second) * normal
            return jnp.where(
                sub < 2, vectors, jnp.where(sub == 3, strip, normal * strip)
            )
        vectors = jnp.where(sub == 0, first, second)
        return jnp.where(sub < 2, vectors, jnp.where(sub == 2, normal * strip, strip))

    def receive(strips, halo, slots, send, recv_halo, recv_slot, is_adjoint):
        def arrival(target, semaphore):
            strip_copy(strips.at[0], target, send.at[0], semaphore, (row, column)).wait_recv()

        for d in range(4):
            @pl.when(~at[d])
            def _():
                arrival(halo.at[d], recv_halo.at[d])

        @pl.when(on_row)
        def _():
            slots[row_slot] = strips[row_edge]

        @pl.when(on_column)
        def _():
            slots[column_slot] = strips[column_edge]

        @pl.when(on_row | on_column)
        def _():
            for slot in range(8):
                mine = (on_row & (row_slot == slot)) | (on_column & (column_slot == slot))

                @pl.when(~mine)
                def _():
                    arrival(slots.at[slot], recv_slot.at[slot])

        @pl.when(on_row)
        def _():
            halo[row_edge] = ghost_across(slots, row_edge, row_part, True, is_adjoint)

        @pl.when(on_column)
        def _():
            halo[column_edge] = ghost_across(
                slots, column_edge, column_part, False, is_adjoint
            )

    def slopes_of(halo, x_fields, y_fields):
        low, high = halo[0], halo[1]
        east = []
        for c, field in enumerate(x_fields):
            before = jnp.where(sub == 0, low[c : c + 1, :], rolled(field, 1, 0))
            after = jnp.where(sub == SUBLANES - 1, high[c : c + 1, :], rolled(field, -1, 0))
            east.append(0.5 * (after - before))
        low = block_transposed(halo[2], sub, inner)
        high = block_transposed(halo[3], sub, inner)
        north = []
        for c, field in enumerate(y_fields):
            before = jnp.where(inner == 0, rolled(low, -c, 1), rolled(field, 1, 1))
            after = jnp.where(
                inner == SUBLANES - 1, rolled(high, SUBLANES - 1 - c, 1), rolled(field, -1, 1)
            )
            north.append(0.5 * (after - before))
        return east, north

    forward = (strips_f, halo_f, slots_f, send_f, recv_halo_f, recv_slot_f)
    adjoint = (strips_a, halo_a, slots_a, send_a, recv_halo_a, recv_slot_a)

    for other in range(faces):
        @pl.when(level <= other)
        def _():
            below_ref[other] = jnp.zeros((SUBLANES, LANES), jnp.float32)

        @pl.when(level > other)
        def _():
            below_copy(other, other).wait_recv()

    pressure = h
    for other in range(faces):
        pressure = pressure + below_ref[other]
    geo = t + heat * pressure
    x_fields, y_fields = (z, m, fx, t, geo), (z, m, fy, t, geo)
    write_strips(strips_f, x_fields, y_fields)
    each_send(*forward, lambda copy: copy.start())
    var_z, var_m, var_h, var_t = [
        per_panel(lambda f, c=c: variance_ref[c, 0, f]) for c in range(4)
    ]
    receive(*forward, False)
    east, north = slopes_of(halo_f, x_fields, y_fields)
    zc = var_z * (z - time_increment * (east[4] + u * east[0] + v * north[0]))
    mc = var_m * (m - time_increment * (north[4] + u * east[1] + v * north[1]))
    hc = var_h * (h - time_increment * (east[2] + north[2]))
    tc = var_t * (t - time_increment * (u * east[3] + v * north[3]))

    x_fields, y_fields = (u * zc, u * mc, zc, hc, u * tc), (v * zc, v * mc, mc, hc, v * tc)
    write_strips(strips_a, x_fields, y_fields)
    each_send(*adjoint, lambda copy: copy.start())
    receive(*adjoint, True)
    east, north = slopes_of(halo_a, x_fields, y_fields)
    geo_back = time_increment * (east[2] + north[2])
    load = heat * geo_back
    column_a[...] = load
    for other in range(faces):
        @pl.when(level > other)
        def _():
            above_copy(other, level).start()

    flux_east = time_increment * east[3]
    flux_north = time_increment * north[3]
    z_back = zc + time_increment * (east[0] + north[0]) + mass * flux_east
    m_back = mc + time_increment * (east[1] + north[1]) + mass * flux_north
    t_back = tc + time_increment * (east[4] + north[4]) + geo_back

    def put(component, tile):
        for p in range(probe_count):
            for f in range(panels):
                start = (p * panels + f) * SUBLANES
                out_ref[p, component, 0, f] = tile[:, start : start + SUBLANES]

    put(0, probe_z + spread_z * z_back)
    put(1, probe_m + spread_m * m_back)
    put(3, probe_t + spread_t * t_back)

    for other in range(faces):
        @pl.when(level >= other)
        def _():
            above_ref[other] = jnp.zeros((SUBLANES, LANES), jnp.float32)

        @pl.when(level < other)
        def _():
            above_copy(other, other).wait_recv()

    for other in range(faces):
        load = load + above_ref[other]
    put(2, probe_h + spread_h * (hc + u * flux_east + v * flux_north + load))

    each_send(*forward, lambda copy: copy.wait_send())
    each_send(*adjoint, lambda copy: copy.wait_send())
    for other in range(faces):
        @pl.when(level < other)
        def _():
            below_copy(other, level).wait_send()

        @pl.when(level > other)
        def _():
            above_copy(other, level).wait_send()


def fused(count, faces, *operands):
    tile = (SUBLANES, LANES)
    vmem = pl.BlockSpec(memory_space=pltpu.VMEM)
    probes = operands[0]
    strips = pltpu.VMEM((4, *tile), jnp.float32)
    slots = pltpu.VMEM((8, *tile), jnp.float32)
    levels = pltpu.VMEM((faces, *tile), jnp.float32)
    one = pltpu.VMEM(tile, jnp.float32)
    dma = pltpu.SemaphoreType.DMA
    return pl.pallas_call(
        functools.partial(tile_kernel, count, faces),
        out_shape=jax.ShapeDtypeStruct(probes.shape, probes.dtype),
        in_specs=[vmem] * 6 + [pl.BlockSpec(memory_space=pltpu.SMEM)],
        out_specs=vmem,
        scratch_shapes=[strips] * 4
        + [slots] * 2
        + [levels] * 2
        + [one] * 2
        + [dma((12,))] * 2
        + [dma((4,))] * 2
        + [dma((8,))] * 2
        + [dma((faces,))] * 4,
        compiler_params=pltpu.CompilerParams(collective_id=0, has_side_effects=True),
    )(*operands)


def solution(mesh):
    count, faces = mesh.shape["tx"], mesh.shape["face"]

    def chosen(*operands):
        probe_count, _, levels, panels, rows, columns = operands[0].shape
        fits = (
            levels == 1
            and count == mesh.shape["ty"]
            and count % 2 == 0
            and rows == columns == SUBLANES
            and probe_count * panels * SUBLANES < LANES
        )
        return fused(count, faces, *operands) if fits else body(*operands)

    return jax.shard_map(
        chosen,
        mesh=mesh,
        in_specs=(
            P(None, None, "face", None, "tx", "ty"),
            P(None, "face", None, "tx", "ty"),
            P("face", None, "tx", "ty"),
            P("face", None, "tx", "ty"),
            P(None, "face", None, "tx", "ty"),
            P(None, "face", None, "tx", "ty"),
            P(),
        ),
        out_specs=P(None, None, "face", None, "tx", "ty"),
        check_vma=False,
    )
```

```python
import functools

import jax
import jax.numpy as jnp
from jax import lax
from jax.experimental import pallas as pl
from jax.experimental.pallas import tpu as pltpu
from jax.sharding import PartitionSpec as P

MESH = pl.DeviceIdType.MESH
SUBLANES = 8
LANES = 128

time_increment = 0.3
forward_layout = (("vector", 0), ("vector", 2), ("scalar", 4), ("scalar", 5))
adjoint_layout = (("tensor", 0), ("vector", 4), ("scalar", 6), ("vector", 7))


def padded_2(array, sides, width):
    for axis, dim in sides:
        devices, length = (lax.axis_size(axis), array.shape[dim])
        up = [(i, (i + 1) % devices) for i in range(devices - 1)]
        down = [(j, i) for i, j in up]
        last = lax.slice_in_dim(array, length - width, length, axis=dim)
        leading = lax.slice_in_dim(array, 0, width, axis=dim)
        before = lax.ppermute(last, axis, up)
        after = lax.ppermute(leading, axis, down)
        array = jnp.concatenate([before, array, after], axis=dim)
    return array


def carried_in(value, axis, join, neutral, backward):
    count, mine = (lax.axis_size(axis), lax.axis_index(axis))
    pieces = lax.all_gather(value, axis)
    if backward:
        pieces = pieces[::-1]
        mine = count - 1 - mine
    total = jnp.full_like(value, 0) + jnp.asarray(neutral, value.dtype)

    def hop(position, total):
        longer = join(total, pieces[position])
        return jnp.where(position < mine, longer, total)

    return lax.fori_loop(0, count - 1, hop, total)


def carry_pair(leading, trailing, entries):
    return (
        entries[0] * leading + entries[1] * trailing,
        entries[2] * leading + entries[3] * trailing,
    )


def rotate_edge(edge_strip, matrix_codes, layout):
    matrix = matrix_codes.astype(edge_strip.dtype)
    entries = [matrix[:, column].reshape(1, 1, 6, 1) for column in range(4)]
    channels = [edge_strip[number] for number in range(edge_strip.shape[0])]
    for species, offset in layout:
        if species == "vector":
            channels[offset], channels[offset + 1] = carry_pair(
                channels[offset], channels[offset + 1], entries
            )
        elif species == "tensor":
            channels[offset], channels[offset + 1] = carry_pair(
                channels[offset], channels[offset + 1], entries
            )
            channels[offset + 2], channels[offset + 3] = carry_pair(
                channels[offset + 2], channels[offset + 3], entries
            )
            channels[offset], channels[offset + 2] = carry_pair(
                channels[offset], channels[offset + 2], entries
            )
            channels[offset + 1], channels[offset + 3] = carry_pair(
                channels[offset + 1], channels[offset + 3], entries
            )
    return jnp.stack(channels)


def orient(edge_rows, face_links, side, layout):
    source_face = face_links[:, side, 0]
    source_edge = face_links[:, side, 1]
    chosen = edge_rows[:, :, :, source_face, source_edge, :]
    flipped = (face_links[:, side, 2] == 1).reshape(1, 1, 1, 6, 1)
    chosen = jnp.where(flipped, chosen[..., ::-1], chosen)
    return rotate_edge(chosen, face_links[:, side, 3:7], layout)


def face_rows(fields):
    tile_row = lax.axis_index("tx")
    tile_column = lax.axis_index("ty")
    low_rows = jnp.where(tile_row == 0, fields[..., 0, :], 0.0)
    high_rows = jnp.where(tile_row == lax.axis_size("tx") - 1, fields[..., -1, :], 0.0)
    low_columns = jnp.where(tile_column == 0, fields[..., :, 0], 0.0)
    high_columns = jnp.where(tile_column == lax.axis_size("ty") - 1, fields[..., :, -1], 0.0)
    row_pair = jnp.stack([low_rows, high_rows], axis=4)
    column_pair = jnp.stack([low_columns, high_columns], axis=4)
    row_full = lax.psum(lax.all_gather(row_pair, "ty", axis=5, tiled=True), "tx")
    column_full = lax.psum(lax.all_gather(column_pair, "tx", axis=5, tiled=True), "ty")
    return jnp.concatenate([row_full, column_full], axis=4)


def extended_slopes(fields, face_links, layout):
    row_cells = fields.shape[4]
    column_cells = fields.shape[5]
    tile_row = lax.axis_index("tx")
    tile_column = lax.axis_index("ty")
    padded = padded_2(fields, (("tx", 4), ("ty", 5)), 1)
    edge_rows = face_rows(fields)
    western = lax.dynamic_slice_in_dim(
        orient(edge_rows, face_links, 0, layout), tile_column * column_cells, column_cells, 4
    )
    eastern = lax.dynamic_slice_in_dim(
        orient(edge_rows, face_links, 1, layout), tile_column * column_cells, column_cells, 4
    )
    southern = lax.dynamic_slice_in_dim(
        orient(edge_rows, face_links, 2, layout), tile_row * row_cells, row_cells, 4
    )
    northern = lax.dynamic_slice_in_dim(
        orient(edge_rows, face_links, 3, layout), tile_row * row_cells, row_cells, 4
    )
    row_number = lax.broadcasted_iota(jnp.int32, (row_cells, column_cells), 0)
    column_number = lax.broadcasted_iota(jnp.int32, (row_cells, column_cells), 1)
    first_row = (row_number == 0) & (tile_row == 0)
    last_row = (row_number == row_cells - 1) & (tile_row == lax.axis_size("tx") - 1)
    first_column = (column_number == 0) & (tile_column == 0)
    last_column = (column_number == column_cells - 1) & (tile_column == lax.axis_size("ty") - 1)
    east_slope_derivative = 0.5 * (padded[..., 2:, 1:-1] - padded[..., :-2, 1:-1])
    east_slope_derivative = (
        east_slope_derivative
        + jnp.where(last_row, 0.5 * eastern[..., None, :], 0.0)
        - jnp.where(first_row, 0.5 * western[..., None, :], 0.0)
    )
    north_slope_derivative = 0.5 * (padded[..., 1:-1, 2:] - padded[..., 1:-1, :-2])
    north_slope_derivative = (
        north_slope_derivative
        + jnp.where(last_column, 0.5 * northern[..., :, None], 0.0)
        - jnp.where(first_column, 0.5 * southern[..., :, None], 0.0)
    )
    return (east_slope_derivative, north_slope_derivative)


def pressure_of(sheet_depth_state):
    within = jnp.cumsum(sheet_depth_state, axis=1)
    totals_here = within[:, -1]
    underneath = carried_in(totals_here, "face", jnp.add, jnp.zeros_like(totals_here), False)
    return within + underneath[:, None]


def load_of(sensitivity):
    within = jnp.flip(jnp.cumsum(jnp.flip(sensitivity, 1), axis=1), 1)
    totals_here = within[:, 0]
    overhead = carried_in(totals_here, "face", jnp.add, jnp.zeros_like(totals_here), True)
    return within + overhead[:, None]


def body(
    probes,
    background_wind,
    layer_mass,
    trajectory_heat_factor,
    spread,
    inverse_misfit_variance,
    face_links,
):
    normalised_state_array = spread[None] * probes
    west_east_wind_part, south_north_wind_speed, sheet_depth_state, sheet_warmth_state = (
        normalised_state_array[:, 0],
        normalised_state_array[:, 1],
        normalised_state_array[:, 2],
        normalised_state_array[:, 3],
    )
    east_wind_speed, north_wind_speed = (background_wind[0], background_wind[1])
    ground_barometric_load = pressure_of(sheet_depth_state)
    gravity_potential_level = sheet_warmth_state + trajectory_heat_factor * ground_barometric_load
    east_mass_transport = east_wind_speed * sheet_depth_state + layer_mass * west_east_wind_part
    north_mass_transport = (
        north_wind_speed * sheet_depth_state + layer_mass * south_north_wind_speed
    )
    joined_state_arrays = jnp.stack(
        [
            west_east_wind_part,
            south_north_wind_speed,
            east_mass_transport,
            north_mass_transport,
            sheet_warmth_state,
            gravity_potential_level,
        ]
    )
    east_slope_derivative, north_slope_derivative = extended_slopes(
        joined_state_arrays, face_links, forward_layout
    )
    west_east_wind_after = west_east_wind_part - time_increment * (
        east_slope_derivative[5]
        + east_wind_speed * east_slope_derivative[0]
        + north_wind_speed * north_slope_derivative[0]
    )
    south_north_wind_after = south_north_wind_speed - time_increment * (
        north_slope_derivative[5]
        + east_wind_speed * east_slope_derivative[1]
        + north_wind_speed * north_slope_derivative[1]
    )
    depth_after_update = sheet_depth_state - time_increment * (
        east_slope_derivative[2] + north_slope_derivative[3]
    )
    warmth_after_update = sheet_warmth_state - time_increment * (
        east_wind_speed * east_slope_derivative[4] + north_wind_speed * north_slope_derivative[4]
    )
    zonal_cost = inverse_misfit_variance[0] * west_east_wind_after
    meridional_cost = inverse_misfit_variance[1] * south_north_wind_after
    thickness_cost = inverse_misfit_variance[2] * depth_after_update
    heat_misfit_penalty = inverse_misfit_variance[3] * warmth_after_update
    sensitive = jnp.stack(
        [
            east_wind_speed * zonal_cost,
            east_wind_speed * meridional_cost,
            north_wind_speed * zonal_cost,
            north_wind_speed * meridional_cost,
            zonal_cost,
            meridional_cost,
            thickness_cost,
            east_wind_speed * heat_misfit_penalty,
            north_wind_speed * heat_misfit_penalty,
        ]
    )
    east_slope_derivative, north_slope_derivative = extended_slopes(
        sensitive, face_links, adjoint_layout
    )
    geo_back = time_increment * (east_slope_derivative[4] + north_slope_derivative[5])
    flux_east_back = time_increment * east_slope_derivative[6]
    flux_north_back = time_increment * north_slope_derivative[6]
    zonal_back = (
        zonal_cost
        + time_increment * (east_slope_derivative[0] + north_slope_derivative[2])
        + layer_mass * flux_east_back
    )
    meridional_back = (
        meridional_cost
        + time_increment * (east_slope_derivative[1] + north_slope_derivative[3])
        + layer_mass * flux_north_back
    )
    warmth_back = (
        heat_misfit_penalty
        + time_increment * (east_slope_derivative[7] + north_slope_derivative[8])
        + geo_back
    )
    thickness_back = (
        thickness_cost
        + east_wind_speed * flux_east_back
        + north_wind_speed * flux_north_back
        + load_of(trajectory_heat_factor * geo_back)
    )
    adjoint_out = jnp.stack([zonal_back, meridional_back, thickness_back, warmth_back], axis=1)
    return probes + spread[None] * adjoint_out


def rolled(tile, shift, axis):
    return pltpu.roll(tile, shift % tile.shape[axis], axis)


def block_transposed(tile, sub, inner):
    step = SUBLANES // 2
    while step:
        ahead = rolled(rolled(tile, -step, 0), step, 1)
        behind = rolled(rolled(tile, step, 0), -step, 1)
        low_row = (sub & step) == 0
        low_lane = (inner & step) == 0
        tile = jnp.where(low_row == low_lane, tile, jnp.where(low_row, ahead, behind))
        step //= 2
    return tile


def block_reversed(tile, inner):
    step = SUBLANES // 2
    while step:
        tile = jnp.where(
            (inner & step) == 0, rolled(tile, -step, 1), rolled(tile, step, 1)
        )
        step //= 2
    return tile


def tile_kernel(
    count,
    faces,
    probes_hbm,
    wind_hbm,
    mass_hbm,
    heat_hbm,
    spread_hbm,
    variance_hbm,
    links_hbm,
    out_hbm,
    probes_ref,
    wind_ref,
    mass_ref,
    heat_ref,
    spread_ref,
    variance_ref,
    links_ref,
    out_ref,
    take_sem,
    put_sem,
    strips_f,
    strips_a,
    halo_f,
    halo_a,
    slots_f,
    slots_a,
    below_ref,
    above_ref,
    column_f,
    column_a,
    send_f,
    send_a,
    recv_halo_f,
    recv_halo_a,
    recv_slot_f,
    recv_slot_a,
    send_below,
    send_above,
    recv_below,
    recv_above,
):
    level = lax.axis_index("face")
    row = lax.axis_index("tx")
    column = lax.axis_index("ty")
    probe_count = probes_ref.shape[0]
    panels = probes_ref.shape[3]
    last = count - 1
    at = [row == 0, row == last, column == 0, column == last]
    on_row = at[0] | at[1]
    on_column = at[2] | at[3]
    corner = on_row & on_column
    middle = (on_row | on_column) & ~corner
    row_edge = jnp.where(at[0], 0, 1)
    column_edge = jnp.where(at[2], 2, 3)
    half = count // 2
    row_part = jnp.where(column < half, 0, 1)
    column_part = jnp.where(row < half, 0, 1)
    row_slot = row_edge * 2 + row_part
    column_slot = column_edge * 2 + column_part
    own_edge = jnp.where(on_row, row_edge, column_edge)
    own_slot = jnp.where(on_row, row_slot, column_slot)
    along = jnp.where(on_row, column, row)
    near = jnp.where(along < half, along, last - along)

    def slot_place(edge, part):
        segment = near if part == 0 else last - near
        return [(0, segment), (last, segment), (segment, 0), (segment, last)][edge]

    beside = [(row - 1, column), (row + 1, column), (row, column - 1), (row, column + 1)]
    corners = [(0, 0), (0, last), (last, 0), (last, last)]

    barrier = pltpu.get_barrier_semaphore()

    def greet(place):
        pl.semaphore_signal(
            barrier,
            inc=1,
            device_id={"tx": place[0], "ty": place[1]},
            device_id_type=MESH,
        )

    for d in range(4):
        @pl.when(~at[d])
        def _():
            greet(beside[d])

    @pl.when(middle)
    def _():
        for slot in range(8):
            @pl.when(own_slot != slot)
            def _():
                greet(slot_place(slot // 2, slot % 2))

    @pl.when(corner)
    def _():
        for place in corners:
            @pl.when((row != place[0]) | (column != place[1]))
            def _():
                greet(place)

    for other in range(faces):
        @pl.when(level != other)
        def _():
            pl.semaphore_signal(
                barrier, inc=1, device_id={"face": other}, device_id_type=MESH
            )

    taken = [
        pltpu.make_async_copy(source, target, take_sem.at[i])
        for i, (source, target) in enumerate(
            (
                (probes_hbm, probes_ref),
                (spread_hbm, spread_ref),
                (wind_hbm, wind_ref),
                (mass_hbm, mass_ref),
                (heat_hbm, heat_ref),
                (variance_hbm, variance_ref),
                (links_hbm, links_ref),
            )
        )
    ]
    for copy in taken:
        copy.start()

    expected = faces - 1 + jnp.where(middle, 7, 0) + jnp.where(corner, 3, 0)
    for d in range(4):
        expected = expected + jnp.where(at[d], 0, 1)

    sub = lax.broadcasted_iota(jnp.int32, (SUBLANES, LANES), 0)
    lane = lax.broadcasted_iota(jnp.int32, (SUBLANES, LANES), 1)
    inner = lane % SUBLANES
    panel_of = (lane // SUBLANES) % panels

    def packed(tiles):
        width = LANES - SUBLANES * len(tiles)
        return jnp.concatenate(tiles + [jnp.zeros((SUBLANES, width), jnp.float32)], axis=1)

    def per_panel(load):
        return packed([load(f) for f in range(panels)] * probe_count)

    def per_probe(component):
        return packed(
            [
                probes_ref[p, component, 0, f]
                for p in range(probe_count)
                for f in range(panels)
            ]
        )

    def level_copy(other, source, target, send, recv):
        return pltpu.make_async_remote_copy(
            src_ref=source,
            dst_ref=target,
            send_sem=send,
            recv_sem=recv,
            device_id={"face": other},
            device_id_type=MESH,
        )

    def below_copy(other, slot):
        return level_copy(
            other, column_f, below_ref.at[slot], send_below.at[other], recv_below.at[slot]
        )

    def above_copy(other, slot):
        return level_copy(
            other, column_a, above_ref.at[slot], send_above.at[other], recv_above.at[slot]
        )

    for copy in taken[:2]:
        copy.wait()
    probe_h = per_probe(2)
    spread_h = per_panel(lambda f: spread_ref[2, 0, f])
    h = spread_h * probe_h
    column_f[...] = h
    pl.semaphore_wait(barrier, expected)
    for other in range(1, faces):
        @pl.when(level < other)
        def _():
            below_copy(other, level).start()

    probe_z, probe_m, probe_t = per_probe(0), per_probe(1), per_probe(3)
    spread_z, spread_m, spread_t = [
        per_panel(lambda f, c=c: spread_ref[c, 0, f]) for c in (0, 1, 3)
    ]
    for copy in taken[2:5]:
        copy.wait()
    u, v = [per_panel(lambda f, c=c: wind_ref[c, 0, f]) for c in range(2)]
    mass = per_panel(lambda f: mass_ref[0, f])
    heat = per_panel(lambda f: heat_ref[0, f])
    z, m, t = spread_z * probe_z, spread_m * probe_m, spread_t * probe_t
    fx = u * h + mass * z
    fy = v * h + mass * m

    def write_strips(strips, x_fields, y_fields):
        low = jnp.zeros((SUBLANES, LANES), jnp.float32)
        high = low
        for c, field in enumerate(x_fields):
            low = jnp.where(sub == c, field[0:1, :], low)
            high = jnp.where(sub == c, field[SUBLANES - 1 : SUBLANES, :], high)
        strips[0] = low
        strips[1] = high
        low = jnp.zeros((SUBLANES, LANES), jnp.float32)
        high = low
        for c, field in enumerate(y_fields):
            low = jnp.where(inner == c, rolled(field, c, 1), low)
            high = jnp.where(inner == c, rolled(field, c - (SUBLANES - 1), 1), high)
        strips[2] = block_transposed(low, sub, inner)
        strips[3] = block_transposed(high, sub, inner)

    def strip_copy(source, target, send, recv, place):
        return pltpu.make_async_remote_copy(
            src_ref=source,
            dst_ref=target,
            send_sem=send,
            recv_sem=recv,
            device_id={"tx": place[0], "ty": place[1]},
            device_id_type=MESH,
        )

    def each_send(strips, halo, slots, send, recv_halo, recv_slot, act):
        @pl.when(middle)
        def _():
            for slot in range(8):
                @pl.when(own_slot != slot)
                def _():
                    act(
                        strip_copy(
                            strips.at[own_edge],
                            slots.at[own_slot],
                            send.at[4 + slot],
                            recv_slot.at[own_slot],
                            slot_place(slot // 2, slot % 2),
                        )
                    )

        @pl.when(corner)
        def _():
            for number, place in enumerate(corners):
                @pl.when((row != place[0]) | (column != place[1]))
                def _():
                    for kind, (edge, slot) in enumerate(
                        ((row_edge, row_slot), (column_edge, column_slot))
                    ):
                        act(
                            strip_copy(
                                strips.at[edge],
                                slots.at[slot],
                                send.at[4 + number * 2 + kind],
                                recv_slot.at[slot],
                                place,
                            )
                        )

        for d in range(4):
            @pl.when(~at[d])
            def _():
                act(
                    strip_copy(
                        strips.at[d],
                        halo.at[d ^ 1],
                        send.at[d],
                        recv_halo.at[d ^ 1],
                        beside[d],
                    )
                )

    def ghost_across(slots, edge, part, is_row, is_adjoint):
        strip = jnp.zeros((SUBLANES, LANES), jnp.float32)
        reverse = jnp.zeros((SUBLANES, LANES), jnp.int32)
        entries = [strip] * 4
        for f in range(panels):
            source = links_ref[f, edge, 0]
            flip = links_ref[f, edge, 2]
            slot = links_ref[f, edge, 1] * 2 + jnp.where(flip == 1, 1 - part, part)
            shift = (SUBLANES * (f - source) + LANES) % LANES
            here = panel_of == f
            strip = jnp.where(here, pltpu.roll(slots[slot], shift, 1), strip)
            reverse = jnp.where(here, flip, reverse)
            entries = [
                jnp.where(here, links_ref[f, edge, 3 + i].astype(jnp.float32), entries[i])
                for i in range(4)
            ]
        strip = jnp.where(reverse == 1, block_reversed(strip, inner), strip)
        m0, m1, m2, m3 = entries
        normal = m0 + m1 if is_row else m2 + m3
        first = m0 * strip + m1 * rolled(strip, -1, 0)
        second = m3 * strip + m2 * rolled(strip, 1, 0)
        if is_adjoint:
            vectors = jnp.where(sub == 0, first, second) * normal
            return jnp.where(
                sub < 2, vectors, jnp.where(sub == 3, strip, normal * strip)
            )
        vectors = jnp.where(sub == 0, first, second)
        return jnp.where(sub < 2, vectors, jnp.where(sub == 2, normal * strip, strip))

    def receive(strips, halo, slots, send, recv_halo, recv_slot, is_adjoint):
        def arrival(target, semaphore):
            strip_copy(strips.at[0], target, send.at[0], semaphore, (row, column)).wait_recv()

        for d in range(4):
            @pl.when(~at[d])
            def _():
                arrival(halo.at[d], recv_halo.at[d])

        @pl.when(on_row)
        def _():
            slots[row_slot] = strips[row_edge]

        @pl.when(on_column)
        def _():
            slots[column_slot] = strips[column_edge]

        @pl.when(on_row | on_column)
        def _():
            for slot in range(8):
                mine = (on_row & (row_slot == slot)) | (on_column & (column_slot == slot))

                @pl.when(~mine)
                def _():
                    arrival(slots.at[slot], recv_slot.at[slot])

        @pl.when(on_row)
        def _():
            halo[row_edge] = ghost_across(slots, row_edge, row_part, True, is_adjoint)

        @pl.when(on_column)
        def _():
            halo[column_edge] = ghost_across(
                slots, column_edge, column_part, False, is_adjoint
            )

    def slopes_of(halo, x_fields, y_fields):
        low, high = halo[0], halo[1]
        east = []
        for c, field in enumerate(x_fields):
            before = jnp.where(sub == 0, low[c : c + 1, :], rolled(field, 1, 0))
            after = jnp.where(sub == SUBLANES - 1, high[c : c + 1, :], rolled(field, -1, 0))
            east.append(0.5 * (after - before))
        low = block_transposed(halo[2], sub, inner)
        high = block_transposed(halo[3], sub, inner)
        north = []
        for c, field in enumerate(y_fields):
            before = jnp.where(inner == 0, rolled(low, -c, 1), rolled(field, 1, 1))
            after = jnp.where(
                inner == SUBLANES - 1, rolled(high, SUBLANES - 1 - c, 1), rolled(field, -1, 1)
            )
            north.append(0.5 * (after - before))
        return east, north

    forward = (strips_f, halo_f, slots_f, send_f, recv_halo_f, recv_slot_f)
    adjoint = (strips_a, halo_a, slots_a, send_a, recv_halo_a, recv_slot_a)

    for other in range(faces):
        @pl.when(level <= other)
        def _():
            below_ref[other] = jnp.zeros((SUBLANES, LANES), jnp.float32)

        @pl.when(level > other)
        def _():
            below_copy(other, other).wait_recv()

    pressure = h
    for other in range(faces):
        pressure = pressure + below_ref[other]
    geo = t + heat * pressure
    x_fields, y_fields = (z, m, fx, t, geo), (z, m, fy, t, geo)
    write_strips(strips_f, x_fields, y_fields)
    each_send(*forward, lambda copy: copy.start())
    for copy in taken[5:]:
        copy.wait()
    var_z, var_m, var_h, var_t = [
        per_panel(lambda f, c=c: variance_ref[c, 0, f]) for c in range(4)
    ]
    receive(*forward, False)
    east, north = slopes_of(halo_f, x_fields, y_fields)
    zc = var_z * (z - time_increment * (east[4] + u * east[0] + v * north[0]))
    mc = var_m * (m - time_increment * (north[4] + u * east[1] + v * north[1]))
    hc = var_h * (h - time_increment * (east[2] + north[2]))
    tc = var_t * (t - time_increment * (u * east[3] + v * north[3]))

    x_fields, y_fields = (u * zc, u * mc, zc, hc, u * tc), (v * zc, v * mc, mc, hc, v * tc)
    write_strips(strips_a, x_fields, y_fields)
    each_send(*adjoint, lambda copy: copy.start())
    receive(*adjoint, True)
    east, north = slopes_of(halo_a, x_fields, y_fields)
    geo_back = time_increment * (east[2] + north[2])
    load = heat * geo_back
    column_a[...] = load
    for other in range(faces):
        @pl.when(level > other)
        def _():
            above_copy(other, level).start()

    flux_east = time_increment * east[3]
    flux_north = time_increment * north[3]
    z_back = zc + time_increment * (east[0] + north[0]) + mass * flux_east
    m_back = mc + time_increment * (east[1] + north[1]) + mass * flux_north
    t_back = tc + time_increment * (east[4] + north[4]) + geo_back

    def put_copy(component, p):
        return pltpu.make_async_copy(
            out_ref.at[component, p], out_hbm.at[p, component, 0], put_sem.at[component, p]
        )

    def put(component, tile):
        for p in range(probe_count):
            for f in range(panels):
                start = (p * panels + f) * SUBLANES
                out_ref[component, p, f] = tile[:, start : start + SUBLANES]
        for p in range(probe_count):
            put_copy(component, p).start()

    put(0, probe_z + spread_z * z_back)
    put(1, probe_m + spread_m * m_back)
    put(3, probe_t + spread_t * t_back)

    for other in range(faces):
        @pl.when(level >= other)
        def _():
            above_ref[other] = jnp.zeros((SUBLANES, LANES), jnp.float32)

        @pl.when(level < other)
        def _():
            above_copy(other, other).wait_recv()

    for other in range(faces):
        load = load + above_ref[other]
    put(2, probe_h + spread_h * (hc + u * flux_east + v * flux_north + load))

    for component in range(4):
        for p in range(probe_count):
            put_copy(component, p).wait()
    each_send(*forward, lambda copy: copy.wait_send())
    each_send(*adjoint, lambda copy: copy.wait_send())
    for other in range(faces):
        @pl.when(level < other)
        def _():
            below_copy(other, level).wait_send()

        @pl.when(level > other)
        def _():
            above_copy(other, level).wait_send()


def fused(count, faces, *operands):
    tile = (SUBLANES, LANES)
    whole = pl.BlockSpec(memory_space=pl.ANY)
    probes = operands[0]
    probe_count, components, _, panels, _, _ = probes.shape
    strips = pltpu.VMEM((4, *tile), jnp.float32)
    slots = pltpu.VMEM((8, *tile), jnp.float32)
    levels = pltpu.VMEM((faces, *tile), jnp.float32)
    one = pltpu.VMEM(tile, jnp.float32)
    dma = pltpu.SemaphoreType.DMA
    return pl.pallas_call(
        functools.partial(tile_kernel, count, faces),
        out_shape=jax.ShapeDtypeStruct(probes.shape, probes.dtype),
        in_specs=[whole] * len(operands),
        out_specs=whole,
        scratch_shapes=[pltpu.VMEM(x.shape, x.dtype) for x in operands[:-1]]
        + [
            pltpu.SMEM(operands[-1].shape, operands[-1].dtype),
            pltpu.VMEM((components, probe_count, panels, SUBLANES, SUBLANES), jnp.float32),
            dma((len(operands),)),
            dma((components, probe_count)),
        ]
        + [strips] * 4
        + [slots] * 2
        + [levels] * 2
        + [one] * 2
        + [dma((12,))] * 2
        + [dma((4,))] * 2
        + [dma((8,))] * 2
        + [dma((faces,))] * 4,
        compiler_params=pltpu.CompilerParams(collective_id=0, has_side_effects=True),
    )(*operands)


def solution(mesh):
    count, faces = mesh.shape["tx"], mesh.shape["face"]

    def chosen(*operands):
        probe_count, _, levels, panels, rows, columns = operands[0].shape
        fits = (
            levels == 1
            and count == mesh.shape["ty"]
            and count % 2 == 0
            and rows == columns == SUBLANES
            and probe_count * panels * SUBLANES < LANES
        )
        return fused(count, faces, *operands) if fits else body(*operands)

    return jax.shard_map(
        chosen,
        mesh=mesh,
        in_specs=(
            P(None, None, "face", None, "tx", "ty"),
            P(None, "face", None, "tx", "ty"),
            P("face", None, "tx", "ty"),
            P("face", None, "tx", "ty"),
            P(None, "face", None, "tx", "ty"),
            P(None, "face", None, "tx", "ty"),
            P(),
        ),
        out_specs=P(None, None, "face", None, "tx", "ty"),
        check_vma=False,
    )
```

```python
import functools

import jax
import jax.numpy as jnp
from jax import lax
from jax.experimental import pallas as pl
from jax.experimental.pallas import tpu as pltpu
from jax.sharding import PartitionSpec as P

MESH = pl.DeviceIdType.MESH
SUBLANES = 8
LANES = 128

time_increment = 0.3
forward_layout = (("vector", 0), ("vector", 2), ("scalar", 4), ("scalar", 5))
adjoint_layout = (("tensor", 0), ("vector", 4), ("scalar", 6), ("vector", 7))


def padded_2(array, sides, width):
    for axis, dim in sides:
        devices, length = (lax.axis_size(axis), array.shape[dim])
        up = [(i, (i + 1) % devices) for i in range(devices - 1)]
        down = [(j, i) for i, j in up]
        last = lax.slice_in_dim(array, length - width, length, axis=dim)
        leading = lax.slice_in_dim(array, 0, width, axis=dim)
        before = lax.ppermute(last, axis, up)
        after = lax.ppermute(leading, axis, down)
        array = jnp.concatenate([before, array, after], axis=dim)
    return array


def carried_in(value, axis, join, neutral, backward):
    count, mine = (lax.axis_size(axis), lax.axis_index(axis))
    pieces = lax.all_gather(value, axis)
    if backward:
        pieces = pieces[::-1]
        mine = count - 1 - mine
    total = jnp.full_like(value, 0) + jnp.asarray(neutral, value.dtype)

    def hop(position, total):
        longer = join(total, pieces[position])
        return jnp.where(position < mine, longer, total)

    return lax.fori_loop(0, count - 1, hop, total)


def carry_pair(leading, trailing, entries):
    return (
        entries[0] * leading + entries[1] * trailing,
        entries[2] * leading + entries[3] * trailing,
    )


def rotate_edge(edge_strip, matrix_codes, layout):
    matrix = matrix_codes.astype(edge_strip.dtype)
    entries = [matrix[:, column].reshape(1, 1, 6, 1) for column in range(4)]
    channels = [edge_strip[number] for number in range(edge_strip.shape[0])]
    for species, offset in layout:
        if species == "vector":
            channels[offset], channels[offset + 1] = carry_pair(
                channels[offset], channels[offset + 1], entries
            )
        elif species == "tensor":
            channels[offset], channels[offset + 1] = carry_pair(
                channels[offset], channels[offset + 1], entries
            )
            channels[offset + 2], channels[offset + 3] = carry_pair(
                channels[offset + 2], channels[offset + 3], entries
            )
            channels[offset], channels[offset + 2] = carry_pair(
                channels[offset], channels[offset + 2], entries
            )
            channels[offset + 1], channels[offset + 3] = carry_pair(
                channels[offset + 1], channels[offset + 3], entries
            )
    return jnp.stack(channels)


def orient(edge_rows, face_links, side, layout):
    source_face = face_links[:, side, 0]
    source_edge = face_links[:, side, 1]
    chosen = edge_rows[:, :, :, source_face, source_edge, :]
    flipped = (face_links[:, side, 2] == 1).reshape(1, 1, 1, 6, 1)
    chosen = jnp.where(flipped, chosen[..., ::-1], chosen)
    return rotate_edge(chosen, face_links[:, side, 3:7], layout)


def face_rows(fields):
    tile_row = lax.axis_index("tx")
    tile_column = lax.axis_index("ty")
    low_rows = jnp.where(tile_row == 0, fields[..., 0, :], 0.0)
    high_rows = jnp.where(tile_row == lax.axis_size("tx") - 1, fields[..., -1, :], 0.0)
    low_columns = jnp.where(tile_column == 0, fields[..., :, 0], 0.0)
    high_columns = jnp.where(tile_column == lax.axis_size("ty") - 1, fields[..., :, -1], 0.0)
    row_pair = jnp.stack([low_rows, high_rows], axis=4)
    column_pair = jnp.stack([low_columns, high_columns], axis=4)
    row_full = lax.psum(lax.all_gather(row_pair, "ty", axis=5, tiled=True), "tx")
    column_full = lax.psum(lax.all_gather(column_pair, "tx", axis=5, tiled=True), "ty")
    return jnp.concatenate([row_full, column_full], axis=4)


def extended_slopes(fields, face_links, layout):
    row_cells = fields.shape[4]
    column_cells = fields.shape[5]
    tile_row = lax.axis_index("tx")
    tile_column = lax.axis_index("ty")
    padded = padded_2(fields, (("tx", 4), ("ty", 5)), 1)
    edge_rows = face_rows(fields)
    western = lax.dynamic_slice_in_dim(
        orient(edge_rows, face_links, 0, layout), tile_column * column_cells, column_cells, 4
    )
    eastern = lax.dynamic_slice_in_dim(
        orient(edge_rows, face_links, 1, layout), tile_column * column_cells, column_cells, 4
    )
    southern = lax.dynamic_slice_in_dim(
        orient(edge_rows, face_links, 2, layout), tile_row * row_cells, row_cells, 4
    )
    northern = lax.dynamic_slice_in_dim(
        orient(edge_rows, face_links, 3, layout), tile_row * row_cells, row_cells, 4
    )
    row_number = lax.broadcasted_iota(jnp.int32, (row_cells, column_cells), 0)
    column_number = lax.broadcasted_iota(jnp.int32, (row_cells, column_cells), 1)
    first_row = (row_number == 0) & (tile_row == 0)
    last_row = (row_number == row_cells - 1) & (tile_row == lax.axis_size("tx") - 1)
    first_column = (column_number == 0) & (tile_column == 0)
    last_column = (column_number == column_cells - 1) & (tile_column == lax.axis_size("ty") - 1)
    east_slope_derivative = 0.5 * (padded[..., 2:, 1:-1] - padded[..., :-2, 1:-1])
    east_slope_derivative = (
        east_slope_derivative
        + jnp.where(last_row, 0.5 * eastern[..., None, :], 0.0)
        - jnp.where(first_row, 0.5 * western[..., None, :], 0.0)
    )
    north_slope_derivative = 0.5 * (padded[..., 1:-1, 2:] - padded[..., 1:-1, :-2])
    north_slope_derivative = (
        north_slope_derivative
        + jnp.where(last_column, 0.5 * northern[..., :, None], 0.0)
        - jnp.where(first_column, 0.5 * southern[..., :, None], 0.0)
    )
    return (east_slope_derivative, north_slope_derivative)


def pressure_of(sheet_depth_state):
    within = jnp.cumsum(sheet_depth_state, axis=1)
    totals_here = within[:, -1]
    underneath = carried_in(totals_here, "face", jnp.add, jnp.zeros_like(totals_here), False)
    return within + underneath[:, None]


def load_of(sensitivity):
    within = jnp.flip(jnp.cumsum(jnp.flip(sensitivity, 1), axis=1), 1)
    totals_here = within[:, 0]
    overhead = carried_in(totals_here, "face", jnp.add, jnp.zeros_like(totals_here), True)
    return within + overhead[:, None]


def body(
    probes,
    background_wind,
    layer_mass,
    trajectory_heat_factor,
    spread,
    inverse_misfit_variance,
    face_links,
):
    normalised_state_array = spread[None] * probes
    west_east_wind_part, south_north_wind_speed, sheet_depth_state, sheet_warmth_state = (
        normalised_state_array[:, 0],
        normalised_state_array[:, 1],
        normalised_state_array[:, 2],
        normalised_state_array[:, 3],
    )
    east_wind_speed, north_wind_speed = (background_wind[0], background_wind[1])
    ground_barometric_load = pressure_of(sheet_depth_state)
    gravity_potential_level = sheet_warmth_state + trajectory_heat_factor * ground_barometric_load
    east_mass_transport = east_wind_speed * sheet_depth_state + layer_mass * west_east_wind_part
    north_mass_transport = (
        north_wind_speed * sheet_depth_state + layer_mass * south_north_wind_speed
    )
    joined_state_arrays = jnp.stack(
        [
            west_east_wind_part,
            south_north_wind_speed,
            east_mass_transport,
            north_mass_transport,
            sheet_warmth_state,
            gravity_potential_level,
        ]
    )
    east_slope_derivative, north_slope_derivative = extended_slopes(
        joined_state_arrays, face_links, forward_layout
    )
    west_east_wind_after = west_east_wind_part - time_increment * (
        east_slope_derivative[5]
        + east_wind_speed * east_slope_derivative[0]
        + north_wind_speed * north_slope_derivative[0]
    )
    south_north_wind_after = south_north_wind_speed - time_increment * (
        north_slope_derivative[5]
        + east_wind_speed * east_slope_derivative[1]
        + north_wind_speed * north_slope_derivative[1]
    )
    depth_after_update = sheet_depth_state - time_increment * (
        east_slope_derivative[2] + north_slope_derivative[3]
    )
    warmth_after_update = sheet_warmth_state - time_increment * (
        east_wind_speed * east_slope_derivative[4] + north_wind_speed * north_slope_derivative[4]
    )
    zonal_cost = inverse_misfit_variance[0] * west_east_wind_after
    meridional_cost = inverse_misfit_variance[1] * south_north_wind_after
    thickness_cost = inverse_misfit_variance[2] * depth_after_update
    heat_misfit_penalty = inverse_misfit_variance[3] * warmth_after_update
    sensitive = jnp.stack(
        [
            east_wind_speed * zonal_cost,
            east_wind_speed * meridional_cost,
            north_wind_speed * zonal_cost,
            north_wind_speed * meridional_cost,
            zonal_cost,
            meridional_cost,
            thickness_cost,
            east_wind_speed * heat_misfit_penalty,
            north_wind_speed * heat_misfit_penalty,
        ]
    )
    east_slope_derivative, north_slope_derivative = extended_slopes(
        sensitive, face_links, adjoint_layout
    )
    geo_back = time_increment * (east_slope_derivative[4] + north_slope_derivative[5])
    flux_east_back = time_increment * east_slope_derivative[6]
    flux_north_back = time_increment * north_slope_derivative[6]
    zonal_back = (
        zonal_cost
        + time_increment * (east_slope_derivative[0] + north_slope_derivative[2])
        + layer_mass * flux_east_back
    )
    meridional_back = (
        meridional_cost
        + time_increment * (east_slope_derivative[1] + north_slope_derivative[3])
        + layer_mass * flux_north_back
    )
    warmth_back = (
        heat_misfit_penalty
        + time_increment * (east_slope_derivative[7] + north_slope_derivative[8])
        + geo_back
    )
    thickness_back = (
        thickness_cost
        + east_wind_speed * flux_east_back
        + north_wind_speed * flux_north_back
        + load_of(trajectory_heat_factor * geo_back)
    )
    adjoint_out = jnp.stack([zonal_back, meridional_back, thickness_back, warmth_back], axis=1)
    return probes + spread[None] * adjoint_out


def rolled(tile, shift, axis):
    return pltpu.roll(tile, shift % tile.shape[axis], axis)


def block_transposed(tile, sub, inner):
    step = SUBLANES // 2
    while step:
        ahead = rolled(rolled(tile, -step, 0), step, 1)
        behind = rolled(rolled(tile, step, 0), -step, 1)
        low_row = (sub & step) == 0
        low_lane = (inner & step) == 0
        tile = jnp.where(low_row == low_lane, tile, jnp.where(low_row, ahead, behind))
        step //= 2
    return tile


def block_reversed(tile, inner):
    step = SUBLANES // 2
    while step:
        tile = jnp.where(
            (inner & step) == 0, rolled(tile, -step, 1), rolled(tile, step, 1)
        )
        step //= 2
    return tile


def tile_kernel(
    count,
    faces,
    probes_hbm,
    wind_hbm,
    mass_hbm,
    heat_hbm,
    spread_hbm,
    variance_hbm,
    links_hbm,
    out_ref,
    probes_ref,
    wind_ref,
    mass_ref,
    heat_ref,
    spread_ref,
    variance_ref,
    links_ref,
    take_sem,
    strips_f,
    strips_a,
    halo_f,
    halo_a,
    slots_f,
    slots_a,
    ghosts,
    below_ref,
    above_ref,
    column_f,
    column_a,
    rows_f,
    rows_a,
    row_halo_f,
    row_halo_a,
    row_slots_f,
    row_slots_a,
    send_f,
    send_a,
    recv_halo_f,
    recv_halo_a,
    recv_slot_f,
    recv_slot_a,
    send_rows_f,
    send_rows_a,
    recv_row_halo_f,
    recv_row_halo_a,
    recv_row_slot_f,
    recv_row_slot_a,
    send_below,
    send_above,
    recv_below,
    recv_above,
):
    level = lax.axis_index("face")
    row = lax.axis_index("tx")
    column = lax.axis_index("ty")
    probe_count = probes_ref.shape[0]
    panels = probes_ref.shape[3]
    last = count - 1
    at = [row == 0, row == last, column == 0, column == last]
    on_row = at[0] | at[1]
    on_column = at[2] | at[3]
    corner = on_row & on_column
    middle = (on_row | on_column) & ~corner
    row_edge = jnp.where(at[0], 0, 1)
    column_edge = jnp.where(at[2], 2, 3)
    half = count // 2
    row_part = jnp.where(column < half, 0, 1)
    column_part = jnp.where(row < half, 0, 1)
    row_slot = row_edge * 2 + row_part
    column_slot = column_edge * 2 + column_part
    own_edge = jnp.where(on_row, row_edge, column_edge)
    own_slot = jnp.where(on_row, row_slot, column_slot)
    along = jnp.where(on_row, column, row)
    near = jnp.where(along < half, along, last - along)

    def slot_place(edge, part):
        segment = near if part == 0 else last - near
        return [(0, segment), (last, segment), (segment, 0), (segment, last)][edge]

    beside = [(row - 1, column), (row + 1, column), (row, column - 1), (row, column + 1)]
    corners = [(0, 0), (0, last), (last, 0), (last, last)]

    barrier = pltpu.get_barrier_semaphore()

    def greet(other, place):
        pl.semaphore_signal(
            barrier,
            inc=1,
            device_id={"face": other, "tx": place[0], "ty": place[1]},
            device_id_type=MESH,
        )

    for other in range(faces):
        for d in range(4):
            @pl.when(~at[d])
            def _():
                greet(other, beside[d])

        @pl.when(middle)
        def _():
            for slot in range(8):
                @pl.when((own_slot != slot) | (level != other))
                def _():
                    greet(other, slot_place(slot // 2, slot % 2))

        @pl.when(corner)
        def _():
            for place in corners:
                @pl.when((row != place[0]) | (column != place[1]) | (level != other))
                def _():
                    greet(other, place)

        @pl.when(level != other)
        def _():
            greet(other, (row, column))

    taken = [
        pltpu.make_async_copy(source, target, take_sem.at[i])
        for i, (source, target) in enumerate(
            (
                (probes_hbm, probes_ref),
                (spread_hbm, spread_ref),
                (wind_hbm, wind_ref),
                (mass_hbm, mass_ref),
                (heat_hbm, heat_ref),
                (variance_hbm, variance_ref),
                (links_hbm, links_ref),
            )
        )
    ]
    for copy in taken:
        copy.start()

    expected = (
        faces - 1 + jnp.where(middle, 8 * faces - 1, 0) + jnp.where(corner, 4 * faces - 1, 0)
    )
    for d in range(4):
        expected = expected + jnp.where(at[d], 0, faces)

    sub = lax.broadcasted_iota(jnp.int32, (SUBLANES, LANES), 0)
    lane = lax.broadcasted_iota(jnp.int32, (SUBLANES, LANES), 1)
    inner = lane % SUBLANES
    panel_of = (lane // SUBLANES) % panels

    def packed(tiles):
        width = LANES - SUBLANES * len(tiles)
        return jnp.concatenate(tiles + [jnp.zeros((SUBLANES, width), jnp.float32)], axis=1)

    def per_panel(load):
        return packed([load(f) for f in range(panels)] * probe_count)

    def per_probe(component):
        return packed(
            [
                probes_ref[p, component, 0, f]
                for p in range(probe_count)
                for f in range(panels)
            ]
        )

    def level_copy(other, source, target, send, recv):
        return pltpu.make_async_remote_copy(
            src_ref=source,
            dst_ref=target,
            send_sem=send,
            recv_sem=recv,
            device_id={"face": other},
            device_id_type=MESH,
        )

    def below_copy(other, slot):
        return level_copy(
            other, column_f, below_ref.at[slot], send_below.at[other], recv_below.at[slot]
        )

    def above_copy(other, slot):
        return level_copy(
            other, column_a, above_ref.at[slot], send_above.at[other], recv_above.at[slot]
        )

    nothing = jnp.zeros((SUBLANES, LANES), jnp.float32)

    def columns_of(y_fields):
        low = high = nothing
        for c, field in enumerate(y_fields):
            low = jnp.where(inner == c, rolled(field, c, 1), low)
            high = jnp.where(inner == c, rolled(field, c - (SUBLANES - 1), 1), high)
        return block_transposed(low, sub, inner), block_transposed(high, sub, inner)

    def write_strips(strips, x_fields, y_fields):
        low = high = nothing
        for c, field in enumerate(x_fields):
            low = jnp.where(sub == c, field[0:1, :], low)
            high = jnp.where(sub == c, field[SUBLANES - 1 : SUBLANES, :], high)
        strips[0] = low
        strips[1] = high
        strips[2], strips[3] = columns_of(y_fields)

    def strip_copy(source, target, send, recv, other, place):
        return pltpu.make_async_remote_copy(
            src_ref=source,
            dst_ref=target,
            send_sem=send,
            recv_sem=recv,
            device_id={"face": other, "tx": place[0], "ty": place[1]},
            device_id_type=MESH,
        )

    def each_send(buffers, act, target=None):
        strips, halo, slots, send, recv_halo, recv_slot = buffers
        across = target is not None
        other = target if across else level
        first_send = 12 * target if across else 0
        first_halo = 4 * level if across else 0
        first_slot = 8 * level if across else 0

        @pl.when(middle)
        def _():
            for slot in range(8):
                @pl.when((own_slot != slot) | across)
                def _():
                    act(
                        strip_copy(
                            strips.at[own_edge],
                            slots.at[first_slot + own_slot],
                            send.at[first_send + 4 + slot],
                            recv_slot.at[first_slot + own_slot],
                            other,
                            slot_place(slot // 2, slot % 2),
                        )
                    )

        @pl.when(corner)
        def _():
            for number, place in enumerate(corners):
                @pl.when((row != place[0]) | (column != place[1]) | across)
                def _():
                    for kind, (edge, slot) in enumerate(
                        ((row_edge, row_slot), (column_edge, column_slot))
                    ):
                        act(
                            strip_copy(
                                strips.at[edge],
                                slots.at[first_slot + slot],
                                send.at[first_send + 4 + number * 2 + kind],
                                recv_slot.at[first_slot + slot],
                                other,
                                place,
                            )
                        )

        for d in range(4):
            @pl.when(~at[d])
            def _():
                act(
                    strip_copy(
                        strips.at[d],
                        halo.at[first_halo + (d ^ 1)],
                        send.at[first_send + d],
                        recv_halo.at[first_halo + (d ^ 1)],
                        other,
                        beside[d],
                    )
                )

    def each_arrival(buffers, source=None):
        strips, halo, slots, send, recv_halo, recv_slot = buffers
        across = source is not None
        first_halo = 4 * source if across else 0
        first_slot = 8 * source if across else 0

        def arrival(target, semaphore):
            strip_copy(
                strips.at[0], target, send.at[0], semaphore, level, (row, column)
            ).wait_recv()

        for d in range(4):
            @pl.when(~at[d])
            def _():
                arrival(halo.at[first_halo + d], recv_halo.at[first_halo + d])

        @pl.when(on_row | on_column)
        def _():
            for slot in range(8):
                mine = (on_row & (row_slot == slot)) | (on_column & (column_slot == slot))

                @pl.when(~mine | across)
                def _():
                    arrival(slots.at[first_slot + slot], recv_slot.at[first_slot + slot])

    forward = (strips_f, halo_f, slots_f, send_f, recv_halo_f, recv_slot_f)
    adjoint = (strips_a, halo_a, slots_a, send_a, recv_halo_a, recv_slot_a)
    forward_rows = (
        rows_f, row_halo_f, row_slots_f, send_rows_f, recv_row_halo_f, recv_row_slot_f
    )
    adjoint_rows = (
        rows_a, row_halo_a, row_slots_a, send_rows_a, recv_row_halo_a, recv_row_slot_a
    )

    def keep_own(strips, slots):
        @pl.when(on_row)
        def _():
            slots[row_slot] = strips[row_edge]

        @pl.when(on_column)
        def _():
            slots[column_slot] = strips[column_edge]

    def with_levels(strip, rows, stride, index, is_adjoint):
        if is_adjoint:
            for other in range(1, faces):
                strip = jnp.where(sub == 4 + other, rows[stride * other + index], strip)
            return strip
        beneath = jnp.zeros((1, LANES), jnp.float32)
        for other in range(faces - 1):
            beneath = beneath + jnp.where(level > other, rows[stride * other + index], 0.0)
        return strip + jnp.where(sub == 4, rolled(strip, -1, 0) * beneath, 0.0)

    def start(copy):
        copy.start()

    def wait_send(copy):
        copy.wait_send()

    for copy in taken[:2]:
        copy.wait()
    probe_h = per_probe(2)
    spread_h = per_panel(lambda f: spread_ref[2, 0, f])
    h = spread_h * probe_h
    column_f[...] = h
    rows_f[0] = h[0:1, :]
    rows_f[1] = h[SUBLANES - 1 : SUBLANES, :]
    low, high = columns_of((h,))
    rows_f[2] = low[0:1, :]
    rows_f[3] = high[0:1, :]
    pl.semaphore_wait(barrier, expected)
    for other in range(1, faces):
        @pl.when(level < other)
        def _():
            each_send(forward_rows, start, other)
            below_copy(other, level).start()

    probe_z, probe_m, probe_t = per_probe(0), per_probe(1), per_probe(3)
    spread_z, spread_m, spread_t = [
        per_panel(lambda f, c=c: spread_ref[c, 0, f]) for c in (0, 1, 3)
    ]
    for copy in taken[2:5]:
        copy.wait()
    u, v = [per_panel(lambda f, c=c: wind_ref[c, 0, f]) for c in range(2)]
    mass = per_panel(lambda f: mass_ref[0, f])
    heat = per_panel(lambda f: heat_ref[0, f])
    z, m, t = spread_z * probe_z, spread_m * probe_m, spread_t * probe_t
    fx = u * h + mass * z
    fy = v * h + mass * m

    def ghost_across(slots, row_slots, edge, part, is_row, is_adjoint):
        strip = jnp.zeros((SUBLANES, LANES), jnp.float32)
        reverse = jnp.zeros((SUBLANES, LANES), jnp.int32)
        entries = [strip] * 4
        for f in range(panels):
            source = links_ref[f, edge, 0]
            flip = links_ref[f, edge, 2]
            slot = links_ref[f, edge, 1] * 2 + jnp.where(flip == 1, 1 - part, part)
            held = with_levels(slots[slot], row_slots, 8, slot, is_adjoint)
            shift = (SUBLANES * (f - source) + LANES) % LANES
            here = panel_of == f
            strip = jnp.where(here, pltpu.roll(held, shift, 1), strip)
            reverse = jnp.where(here, flip, reverse)
            entries = [
                jnp.where(here, links_ref[f, edge, 3 + i].astype(jnp.float32), entries[i])
                for i in range(4)
            ]
        strip = jnp.where(reverse == 1, block_reversed(strip, inner), strip)
        m0, m1, m2, m3 = entries
        normal = m0 + m1 if is_row else m2 + m3
        first = m0 * strip + m1 * rolled(strip, -1, 0)
        second = m3 * strip + m2 * rolled(strip, 1, 0)
        if is_adjoint:
            vectors = jnp.where(sub == 0, first, second) * normal
            return jnp.where(
                sub < 2, vectors, jnp.where(sub == 3, strip, normal * strip)
            )
        vectors = jnp.where(sub == 0, first, second)
        return jnp.where(sub < 2, vectors, jnp.where(sub == 2, normal * strip, strip))

    def make_ghosts(buffers, rows_buffers, is_adjoint):
        strips, halo, slots = buffers[:3]
        row_halo, row_slots = rows_buffers[1:3]
        for d in range(4):
            @pl.when(~at[d])
            def _():
                ghosts[d] = with_levels(halo[d], row_halo, 4, d, is_adjoint)

        @pl.when(on_row)
        def _():
            ghosts[row_edge] = ghost_across(
                slots, row_slots, row_edge, row_part, True, is_adjoint
            )

        @pl.when(on_column)
        def _():
            ghosts[column_edge] = ghost_across(
                slots, row_slots, column_edge, column_part, False, is_adjoint
            )

    def slopes_of(x_fields, y_fields):
        low, high = ghosts[0], ghosts[1]
        east = []
        for c, field in enumerate(x_fields):
            before = jnp.where(sub == 0, low[c : c + 1, :], rolled(field, 1, 0))
            after = jnp.where(sub == SUBLANES - 1, high[c : c + 1, :], rolled(field, -1, 0))
            east.append(0.5 * (after - before))
        low = block_transposed(ghosts[2], sub, inner)
        high = block_transposed(ghosts[3], sub, inner)
        north = []
        for c, field in enumerate(y_fields):
            before = jnp.where(inner == 0, rolled(low, -c, 1), rolled(field, 1, 1))
            after = jnp.where(
                inner == SUBLANES - 1, rolled(high, SUBLANES - 1 - c, 1), rolled(field, -1, 1)
            )
            north.append(0.5 * (after - before))
        return east, north

    geo = t + heat * h
    write_strips(strips_f, (z, m, fx, t, geo, heat), (z, m, fy, t, geo, heat))
    each_send(forward, start)
    keep_own(strips_f, slots_f)
    for copy in taken[5:]:
        copy.wait()
    var_z, var_m, var_h, var_t = [
        per_panel(lambda f, c=c: variance_ref[c, 0, f]) for c in range(4)
    ]
    each_arrival(forward)
    for other in range(faces - 1):
        @pl.when(level > other)
        def _():
            below_copy(other, other).wait_recv()
            each_arrival(forward_rows, other)

    for other in range(faces - 1):
        geo = geo + heat * jnp.where(level > other, below_ref[other], 0.0)
    make_ghosts(forward, forward_rows, False)
    east, north = slopes_of((z, m, fx, t, geo), (z, m, fy, t, geo))
    zc = var_z * (z - time_increment * (east[4] + u * east[0] + v * north[0]))
    mc = var_m * (m - time_increment * (north[4] + u * east[1] + v * north[1]))
    hc = var_h * (h - time_increment * (east[2] + north[2]))
    tc = var_t * (t - time_increment * (u * east[3] + v * north[3]))

    x_fields, y_fields = (u * zc, u * mc, zc, hc, u * tc), (v * zc, v * mc, mc, hc, v * tc)
    write_strips(strips_a, x_fields, y_fields)
    for d in range(4):
        rows_a[d] = strips_a[d][2:3, :]
    column_a[0], column_a[1], column_a[2] = zc, mc, heat
    for other in range(faces):
        @pl.when(level > other)
        def _():
            each_send(adjoint_rows, start, other)

    each_send(adjoint, start)
    for other in range(faces):
        @pl.when(level > other)
        def _():
            above_copy(other, level).start()

    keep_own(strips_a, slots_a)
    each_arrival(adjoint)
    for other in range(1, faces):
        @pl.when(level < other)
        def _():
            above_copy(other, other).wait_recv()
            each_arrival(adjoint_rows, other)

    make_ghosts(adjoint, adjoint_rows, True)
    above = [above_ref[other] for other in range(1, faces)]
    east, north = slopes_of(
        x_fields + tuple(tiles[0] for tiles in above),
        y_fields + tuple(tiles[1] for tiles in above),
    )
    geo_back = time_increment * (east[2] + north[2])
    load = heat * geo_back
    for other, tiles in enumerate(above, 1):
        upper = tiles[2] * (time_increment * (east[4 + other] + north[4 + other]))
        load = load + jnp.where(level < other, upper, 0.0)

    flux_east = time_increment * east[3]
    flux_north = time_increment * north[3]
    z_back = zc + time_increment * (east[0] + north[0]) + mass * flux_east
    m_back = mc + time_increment * (east[1] + north[1]) + mass * flux_north
    t_back = tc + time_increment * (east[4] + north[4]) + geo_back
    h_back = hc + u * flux_east + v * flux_north + load
    out_ref[0] = probe_z + spread_z * z_back
    out_ref[1] = probe_m + spread_m * m_back
    out_ref[2] = probe_h + spread_h * h_back
    out_ref[3] = probe_t + spread_t * t_back

    each_send(forward, wait_send)
    each_send(adjoint, wait_send)
    for other in range(faces):
        @pl.when(level < other)
        def _():
            each_send(forward_rows, wait_send, other)
            below_copy(other, level).wait_send()

        @pl.when(level > other)
        def _():
            each_send(adjoint_rows, wait_send, other)
            above_copy(other, level).wait_send()


def unpack_kernel(packed_ref, out_ref):
    probe_count, components, _, panels, _, _ = out_ref.shape
    for component in range(components):
        tile = packed_ref[component]
        for p in range(probe_count):
            for f in range(panels):
                start = (p * panels + f) * SUBLANES
                out_ref[p, component, 0, f] = tile[:, start : start + SUBLANES]


def fused(count, faces, *operands):
    tile = (SUBLANES, LANES)
    vmem = pl.BlockSpec(memory_space=pltpu.VMEM)
    whole = pl.BlockSpec(memory_space=pl.ANY)
    probes = operands[0]
    strips = pltpu.VMEM((4, *tile), jnp.float32)
    slots = pltpu.VMEM((8, *tile), jnp.float32)

    def edge_rows(number):
        return pltpu.VMEM((number, 1, LANES), jnp.float32)

    dma = pltpu.SemaphoreType.DMA
    packed = pl.pallas_call(
        functools.partial(tile_kernel, count, faces),
        out_shape=jax.ShapeDtypeStruct((probes.shape[1], *tile), probes.dtype),
        in_specs=[whole] * len(operands),
        out_specs=vmem,
        scratch_shapes=[pltpu.VMEM(x.shape, x.dtype) for x in operands[:-1]]
        + [
            pltpu.SMEM(operands[-1].shape, operands[-1].dtype),
            dma((len(operands),)),
        ]
        + [strips] * 4
        + [slots] * 2
        + [strips]
        + [pltpu.VMEM((faces, *tile), jnp.float32), pltpu.VMEM((faces, 3, *tile), jnp.float32)]
        + [pltpu.VMEM(tile, jnp.float32), pltpu.VMEM((3, *tile), jnp.float32)]
        + [edge_rows(4)] * 2
        + [edge_rows(4 * faces)] * 2
        + [edge_rows(8 * faces)] * 2
        + [dma((12,))] * 2
        + [dma((4,))] * 2
        + [dma((8,))] * 2
        + [dma((12 * faces,))] * 2
        + [dma((4 * faces,))] * 2
        + [dma((8 * faces,))] * 2
        + [dma((faces,))] * 4,
        compiler_params=pltpu.CompilerParams(collective_id=0, has_side_effects=True),
    )(*operands)
    return pl.pallas_call(
        unpack_kernel,
        out_shape=jax.ShapeDtypeStruct(probes.shape, probes.dtype),
        in_specs=[vmem],
        out_specs=vmem,
    )(packed)


def solution(mesh):
    count, faces = mesh.shape["tx"], mesh.shape["face"]

    def chosen(*operands):
        probe_count, _, levels, panels, rows, columns = operands[0].shape
        fits = (
            levels == 1
            and count == mesh.shape["ty"]
            and count % 2 == 0
            and rows == columns == SUBLANES
            and faces + 4 <= SUBLANES
            and probe_count * panels * SUBLANES < LANES
        )
        return fused(count, faces, *operands) if fits else body(*operands)

    return jax.shard_map(
        chosen,
        mesh=mesh,
        in_specs=(
            P(None, None, "face", None, "tx", "ty"),
            P(None, "face", None, "tx", "ty"),
            P("face", None, "tx", "ty"),
            P("face", None, "tx", "ty"),
            P(None, "face", None, "tx", "ty"),
            P(None, "face", None, "tx", "ty"),
            P(),
        ),
        out_specs=P(None, None, "face", None, "tx", "ty"),
        check_vma=False,
    )
```

```python
import functools

import jax
import jax.numpy as jnp
from jax import lax
from jax.experimental import pallas as pl
from jax.experimental.pallas import tpu as pltpu
from jax.sharding import PartitionSpec as P

MESH = pl.DeviceIdType.MESH
SUBLANES = 8
LANES = 128
VMEM_BYTES = 4 * 2**20

time_increment = 0.3
forward_layout = (("vector", 0), ("vector", 2), ("scalar", 4), ("scalar", 5))
adjoint_layout = (("tensor", 0), ("vector", 4), ("scalar", 6), ("vector", 7))


def padded_2(array, sides, width):
    for axis, dim in sides:
        devices, length = (lax.axis_size(axis), array.shape[dim])
        up = [(i, (i + 1) % devices) for i in range(devices - 1)]
        down = [(j, i) for i, j in up]
        last = lax.slice_in_dim(array, length - width, length, axis=dim)
        leading = lax.slice_in_dim(array, 0, width, axis=dim)
        before = lax.ppermute(last, axis, up)
        after = lax.ppermute(leading, axis, down)
        array = jnp.concatenate([before, array, after], axis=dim)
    return array


def carried_in(value, axis, join, neutral, backward):
    count, mine = (lax.axis_size(axis), lax.axis_index(axis))
    pieces = lax.all_gather(value, axis)
    if backward:
        pieces = pieces[::-1]
        mine = count - 1 - mine
    total = jnp.full_like(value, 0) + jnp.asarray(neutral, value.dtype)

    def hop(position, total):
        longer = join(total, pieces[position])
        return jnp.where(position < mine, longer, total)

    return lax.fori_loop(0, count - 1, hop, total)


def carry_pair(leading, trailing, entries):
    return (
        entries[0] * leading + entries[1] * trailing,
        entries[2] * leading + entries[3] * trailing,
    )


def rotate_edge(edge_strip, matrix_codes, layout):
    matrix = matrix_codes.astype(edge_strip.dtype)
    entries = [matrix[:, column].reshape(1, 1, 6, 1) for column in range(4)]
    channels = [edge_strip[number] for number in range(edge_strip.shape[0])]
    for species, offset in layout:
        if species == "vector":
            channels[offset], channels[offset + 1] = carry_pair(
                channels[offset], channels[offset + 1], entries
            )
        elif species == "tensor":
            channels[offset], channels[offset + 1] = carry_pair(
                channels[offset], channels[offset + 1], entries
            )
            channels[offset + 2], channels[offset + 3] = carry_pair(
                channels[offset + 2], channels[offset + 3], entries
            )
            channels[offset], channels[offset + 2] = carry_pair(
                channels[offset], channels[offset + 2], entries
            )
            channels[offset + 1], channels[offset + 3] = carry_pair(
                channels[offset + 1], channels[offset + 3], entries
            )
    return jnp.stack(channels)


def orient(edge_rows, face_links, side, layout):
    source_face = face_links[:, side, 0]
    source_edge = face_links[:, side, 1]
    chosen = edge_rows[:, :, :, source_face, source_edge, :]
    flipped = (face_links[:, side, 2] == 1).reshape(1, 1, 1, 6, 1)
    chosen = jnp.where(flipped, chosen[..., ::-1], chosen)
    return rotate_edge(chosen, face_links[:, side, 3:7], layout)


def face_rows(fields):
    tile_row = lax.axis_index("tx")
    tile_column = lax.axis_index("ty")
    low_rows = jnp.where(tile_row == 0, fields[..., 0, :], 0.0)
    high_rows = jnp.where(tile_row == lax.axis_size("tx") - 1, fields[..., -1, :], 0.0)
    low_columns = jnp.where(tile_column == 0, fields[..., :, 0], 0.0)
    high_columns = jnp.where(tile_column == lax.axis_size("ty") - 1, fields[..., :, -1], 0.0)
    row_pair = jnp.stack([low_rows, high_rows], axis=4)
    column_pair = jnp.stack([low_columns, high_columns], axis=4)
    row_full = lax.psum(lax.all_gather(row_pair, "ty", axis=5, tiled=True), "tx")
    column_full = lax.psum(lax.all_gather(column_pair, "tx", axis=5, tiled=True), "ty")
    return jnp.concatenate([row_full, column_full], axis=4)


def extended_slopes(fields, face_links, layout):
    row_cells = fields.shape[4]
    column_cells = fields.shape[5]
    tile_row = lax.axis_index("tx")
    tile_column = lax.axis_index("ty")
    padded = padded_2(fields, (("tx", 4), ("ty", 5)), 1)
    edge_rows = face_rows(fields)
    western = lax.dynamic_slice_in_dim(
        orient(edge_rows, face_links, 0, layout), tile_column * column_cells, column_cells, 4
    )
    eastern = lax.dynamic_slice_in_dim(
        orient(edge_rows, face_links, 1, layout), tile_column * column_cells, column_cells, 4
    )
    southern = lax.dynamic_slice_in_dim(
        orient(edge_rows, face_links, 2, layout), tile_row * row_cells, row_cells, 4
    )
    northern = lax.dynamic_slice_in_dim(
        orient(edge_rows, face_links, 3, layout), tile_row * row_cells, row_cells, 4
    )
    row_number = lax.broadcasted_iota(jnp.int32, (row_cells, column_cells), 0)
    column_number = lax.broadcasted_iota(jnp.int32, (row_cells, column_cells), 1)
    first_row = (row_number == 0) & (tile_row == 0)
    last_row = (row_number == row_cells - 1) & (tile_row == lax.axis_size("tx") - 1)
    first_column = (column_number == 0) & (tile_column == 0)
    last_column = (column_number == column_cells - 1) & (tile_column == lax.axis_size("ty") - 1)
    east_slope_derivative = 0.5 * (padded[..., 2:, 1:-1] - padded[..., :-2, 1:-1])
    east_slope_derivative = (
        east_slope_derivative
        + jnp.where(last_row, 0.5 * eastern[..., None, :], 0.0)
        - jnp.where(first_row, 0.5 * western[..., None, :], 0.0)
    )
    north_slope_derivative = 0.5 * (padded[..., 1:-1, 2:] - padded[..., 1:-1, :-2])
    north_slope_derivative = (
        north_slope_derivative
        + jnp.where(last_column, 0.5 * northern[..., :, None], 0.0)
        - jnp.where(first_column, 0.5 * southern[..., :, None], 0.0)
    )
    return (east_slope_derivative, north_slope_derivative)


def pressure_of(sheet_depth_state):
    within = jnp.cumsum(sheet_depth_state, axis=1)
    totals_here = within[:, -1]
    underneath = carried_in(totals_here, "face", jnp.add, jnp.zeros_like(totals_here), False)
    return within + underneath[:, None]


def load_of(sensitivity):
    within = jnp.flip(jnp.cumsum(jnp.flip(sensitivity, 1), axis=1), 1)
    totals_here = within[:, 0]
    overhead = carried_in(totals_here, "face", jnp.add, jnp.zeros_like(totals_here), True)
    return within + overhead[:, None]


def body(
    probes,
    background_wind,
    layer_mass,
    trajectory_heat_factor,
    spread,
    inverse_misfit_variance,
    face_links,
):
    normalised_state_array = spread[None] * probes
    west_east_wind_part, south_north_wind_speed, sheet_depth_state, sheet_warmth_state = (
        normalised_state_array[:, 0],
        normalised_state_array[:, 1],
        normalised_state_array[:, 2],
        normalised_state_array[:, 3],
    )
    east_wind_speed, north_wind_speed = (background_wind[0], background_wind[1])
    ground_barometric_load = pressure_of(sheet_depth_state)
    gravity_potential_level = sheet_warmth_state + trajectory_heat_factor * ground_barometric_load
    east_mass_transport = east_wind_speed * sheet_depth_state + layer_mass * west_east_wind_part
    north_mass_transport = (
        north_wind_speed * sheet_depth_state + layer_mass * south_north_wind_speed
    )
    joined_state_arrays = jnp.stack(
        [
            west_east_wind_part,
            south_north_wind_speed,
            east_mass_transport,
            north_mass_transport,
            sheet_warmth_state,
            gravity_potential_level,
        ]
    )
    east_slope_derivative, north_slope_derivative = extended_slopes(
        joined_state_arrays, face_links, forward_layout
    )
    west_east_wind_after = west_east_wind_part - time_increment * (
        east_slope_derivative[5]
        + east_wind_speed * east_slope_derivative[0]
        + north_wind_speed * north_slope_derivative[0]
    )
    south_north_wind_after = south_north_wind_speed - time_increment * (
        north_slope_derivative[5]
        + east_wind_speed * east_slope_derivative[1]
        + north_wind_speed * north_slope_derivative[1]
    )
    depth_after_update = sheet_depth_state - time_increment * (
        east_slope_derivative[2] + north_slope_derivative[3]
    )
    warmth_after_update = sheet_warmth_state - time_increment * (
        east_wind_speed * east_slope_derivative[4] + north_wind_speed * north_slope_derivative[4]
    )
    zonal_cost = inverse_misfit_variance[0] * west_east_wind_after
    meridional_cost = inverse_misfit_variance[1] * south_north_wind_after
    thickness_cost = inverse_misfit_variance[2] * depth_after_update
    heat_misfit_penalty = inverse_misfit_variance[3] * warmth_after_update
    sensitive = jnp.stack(
        [
            east_wind_speed * zonal_cost,
            east_wind_speed * meridional_cost,
            north_wind_speed * zonal_cost,
            north_wind_speed * meridional_cost,
            zonal_cost,
            meridional_cost,
            thickness_cost,
            east_wind_speed * heat_misfit_penalty,
            north_wind_speed * heat_misfit_penalty,
        ]
    )
    east_slope_derivative, north_slope_derivative = extended_slopes(
        sensitive, face_links, adjoint_layout
    )
    geo_back = time_increment * (east_slope_derivative[4] + north_slope_derivative[5])
    flux_east_back = time_increment * east_slope_derivative[6]
    flux_north_back = time_increment * north_slope_derivative[6]
    zonal_back = (
        zonal_cost
        + time_increment * (east_slope_derivative[0] + north_slope_derivative[2])
        + layer_mass * flux_east_back
    )
    meridional_back = (
        meridional_cost
        + time_increment * (east_slope_derivative[1] + north_slope_derivative[3])
        + layer_mass * flux_north_back
    )
    warmth_back = (
        heat_misfit_penalty
        + time_increment * (east_slope_derivative[7] + north_slope_derivative[8])
        + geo_back
    )
    thickness_back = (
        thickness_cost
        + east_wind_speed * flux_east_back
        + north_wind_speed * flux_north_back
        + load_of(trajectory_heat_factor * geo_back)
    )
    adjoint_out = jnp.stack([zonal_back, meridional_back, thickness_back, warmth_back], axis=1)
    return probes + spread[None] * adjoint_out


def rolled(tile, shift, axis):
    return pltpu.roll(tile, shift % tile.shape[axis], axis)


def block_transposed(tile, sub, inner):
    step = SUBLANES // 2
    while step:
        ahead = rolled(rolled(tile, -step, 0), step, 1)
        behind = rolled(rolled(tile, step, 0), -step, 1)
        low_row = (sub & step) == 0
        low_lane = (inner & step) == 0
        tile = jnp.where(low_row == low_lane, tile, jnp.where(low_row, ahead, behind))
        step //= 2
    return tile


def block_reversed(tile, inner):
    step = SUBLANES // 2
    while step:
        tile = jnp.where(
            (inner & step) == 0, rolled(tile, -step, 1), rolled(tile, step, 1)
        )
        step //= 2
    return tile


def tile_kernel(
    count,
    faces,
    probes_hbm,
    wind_hbm,
    mass_hbm,
    heat_hbm,
    spread_hbm,
    variance_hbm,
    links_hbm,
    out_ref,
    probes_ref,
    wind_ref,
    mass_ref,
    heat_ref,
    spread_ref,
    variance_ref,
    links_ref,
    take_sem,
    strips_f,
    strips_a,
    halo_f,
    halo_a,
    slots_f,
    slots_a,
    ghosts,
    below_ref,
    above_ref,
    column_f,
    column_a,
    rows_f,
    rows_a,
    row_halo_f,
    row_halo_a,
    row_slots_f,
    row_slots_a,
    send_f,
    send_a,
    recv_halo_f,
    recv_halo_a,
    recv_slot_f,
    recv_slot_a,
    send_rows_f,
    send_rows_a,
    recv_row_halo_f,
    recv_row_halo_a,
    recv_row_slot_f,
    recv_row_slot_a,
    send_below,
    send_above,
    recv_below,
    recv_above,
):
    level = lax.axis_index("face")
    row = lax.axis_index("tx")
    column = lax.axis_index("ty")
    probe_count = probes_ref.shape[0]
    panels = probes_ref.shape[3]
    last = count - 1
    at = [row == 0, row == last, column == 0, column == last]
    on_row = at[0] | at[1]
    on_column = at[2] | at[3]
    corner = on_row & on_column
    middle = (on_row | on_column) & ~corner
    row_edge = jnp.where(at[0], 0, 1)
    column_edge = jnp.where(at[2], 2, 3)
    half = count // 2
    row_part = jnp.where(column < half, 0, 1)
    column_part = jnp.where(row < half, 0, 1)
    row_slot = row_edge * 2 + row_part
    column_slot = column_edge * 2 + column_part
    own_edge = jnp.where(on_row, row_edge, column_edge)
    own_slot = jnp.where(on_row, row_slot, column_slot)
    along = jnp.where(on_row, column, row)
    near = jnp.where(along < half, along, last - along)

    def slot_place(edge, part):
        segment = near if part == 0 else last - near
        return [(0, segment), (last, segment), (segment, 0), (segment, last)][edge]

    beside = [(row - 1, column), (row + 1, column), (row, column - 1), (row, column + 1)]
    corners = [(0, 0), (0, last), (last, 0), (last, last)]

    barrier = pltpu.get_barrier_semaphore()

    def greet(other, place):
        pl.semaphore_signal(
            barrier,
            inc=1,
            device_id={"face": other, "tx": place[0], "ty": place[1]},
            device_id_type=MESH,
        )

    for other in range(faces):
        for d in range(4):
            @pl.when(~at[d])
            def _():
                greet(other, beside[d])

        @pl.when(middle)
        def _():
            for slot in range(8):
                @pl.when((own_slot != slot) | (level != other))
                def _():
                    greet(other, slot_place(slot // 2, slot % 2))

        @pl.when(corner)
        def _():
            for place in corners:
                @pl.when((row != place[0]) | (column != place[1]) | (level != other))
                def _():
                    greet(other, place)

        @pl.when(level != other)
        def _():
            greet(other, (row, column))

    taken = [
        pltpu.make_async_copy(source, target, take_sem.at[i])
        for i, (source, target) in enumerate(
            (
                (probes_hbm, probes_ref),
                (spread_hbm, spread_ref),
                (wind_hbm, wind_ref),
                (mass_hbm, mass_ref),
                (heat_hbm, heat_ref),
                (variance_hbm, variance_ref),
                (links_hbm, links_ref),
            )
        )
    ]
    for copy in taken:
        copy.start()

    expected = (
        faces - 1 + jnp.where(middle, 8 * faces - 1, 0) + jnp.where(corner, 4 * faces - 1, 0)
    )
    for d in range(4):
        expected = expected + jnp.where(at[d], 0, faces)

    sub = lax.broadcasted_iota(jnp.int32, (SUBLANES, LANES), 0)
    lane = lax.broadcasted_iota(jnp.int32, (SUBLANES, LANES), 1)
    inner = lane % SUBLANES
    panel_of = (lane // SUBLANES) % panels

    def packed(tiles):
        width = LANES - SUBLANES * len(tiles)
        return jnp.concatenate(tiles + [jnp.zeros((SUBLANES, width), jnp.float32)], axis=1)

    def per_panel(load):
        return packed([load(f) for f in range(panels)] * probe_count)

    def per_probe(component):
        return packed(
            [
                probes_ref[p, component, 0, f]
                for p in range(probe_count)
                for f in range(panels)
            ]
        )

    def level_copy(other, source, target, send, recv):
        return pltpu.make_async_remote_copy(
            src_ref=source,
            dst_ref=target,
            send_sem=send,
            recv_sem=recv,
            device_id={"face": other},
            device_id_type=MESH,
        )

    def below_copy(other, slot):
        return level_copy(
            other, column_f, below_ref.at[slot], send_below.at[other], recv_below.at[slot]
        )

    def above_copy(other, slot):
        return level_copy(
            other, column_a, above_ref.at[slot], send_above.at[other], recv_above.at[slot]
        )

    nothing = jnp.zeros((SUBLANES, LANES), jnp.float32)

    def columns_of(y_fields):
        low = high = nothing
        for c, field in enumerate(y_fields):
            low = jnp.where(inner == c, rolled(field, c, 1), low)
            high = jnp.where(inner == c, rolled(field, c - (SUBLANES - 1), 1), high)
        return block_transposed(low, sub, inner), block_transposed(high, sub, inner)

    def write_strips(strips, x_fields, y_fields):
        low = high = nothing
        for c, field in enumerate(x_fields):
            low = jnp.where(sub == c, field[0:1, :], low)
            high = jnp.where(sub == c, field[SUBLANES - 1 : SUBLANES, :], high)
        strips[0] = low
        strips[1] = high
        strips[2], strips[3] = columns_of(y_fields)

    def strip_copy(source, target, send, recv, other, place):
        return pltpu.make_async_remote_copy(
            src_ref=source,
            dst_ref=target,
            send_sem=send,
            recv_sem=recv,
            device_id={"face": other, "tx": place[0], "ty": place[1]},
            device_id_type=MESH,
        )

    def each_send(buffers, act, target=None):
        strips, halo, slots, send, recv_halo, recv_slot = buffers
        across = target is not None
        other = target if across else level
        first_send = 12 * target if across else 0
        first_halo = 4 * level if across else 0
        first_slot = 8 * level if across else 0

        @pl.when(middle)
        def _():
            for slot in range(8):
                @pl.when((own_slot != slot) | across)
                def _():
                    act(
                        strip_copy(
                            strips.at[own_edge],
                            slots.at[first_slot + own_slot],
                            send.at[first_send + 4 + slot],
                            recv_slot.at[first_slot + own_slot],
                            other,
                            slot_place(slot // 2, slot % 2),
                        )
                    )

        @pl.when(corner)
        def _():
            for number, place in enumerate(corners):
                @pl.when((row != place[0]) | (column != place[1]) | across)
                def _():
                    for kind, (edge, slot) in enumerate(
                        ((row_edge, row_slot), (column_edge, column_slot))
                    ):
                        act(
                            strip_copy(
                                strips.at[edge],
                                slots.at[first_slot + slot],
                                send.at[first_send + 4 + number * 2 + kind],
                                recv_slot.at[first_slot + slot],
                                other,
                                place,
                            )
                        )

        for d in range(4):
            @pl.when(~at[d])
            def _():
                act(
                    strip_copy(
                        strips.at[d],
                        halo.at[first_halo + (d ^ 1)],
                        send.at[first_send + d],
                        recv_halo.at[first_halo + (d ^ 1)],
                        other,
                        beside[d],
                    )
                )

    def each_arrival(buffers, source=None):
        strips, halo, slots, send, recv_halo, recv_slot = buffers
        across = source is not None
        first_halo = 4 * source if across else 0
        first_slot = 8 * source if across else 0

        def arrival(target, semaphore):
            strip_copy(
                strips.at[0], target, send.at[0], semaphore, level, (row, column)
            ).wait_recv()

        for d in range(4):
            @pl.when(~at[d])
            def _():
                arrival(halo.at[first_halo + d], recv_halo.at[first_halo + d])

        @pl.when(on_row | on_column)
        def _():
            for slot in range(8):
                mine = (on_row & (row_slot == slot)) | (on_column & (column_slot == slot))

                @pl.when(~mine | across)
                def _():
                    arrival(slots.at[first_slot + slot], recv_slot.at[first_slot + slot])

    forward = (strips_f, halo_f, slots_f, send_f, recv_halo_f, recv_slot_f)
    adjoint = (strips_a, halo_a, slots_a, send_a, recv_halo_a, recv_slot_a)
    forward_rows = (
        rows_f, row_halo_f, row_slots_f, send_rows_f, recv_row_halo_f, recv_row_slot_f
    )
    adjoint_rows = (
        rows_a, row_halo_a, row_slots_a, send_rows_a, recv_row_halo_a, recv_row_slot_a
    )

    def keep_own(strips, slots):
        @pl.when(on_row)
        def _():
            slots[row_slot] = strips[row_edge]

        @pl.when(on_column)
        def _():
            slots[column_slot] = strips[column_edge]

    def with_levels(strip, rows, stride, index, is_adjoint):
        if is_adjoint:
            for other in range(1, faces):
                strip = jnp.where(sub == 4 + other, rows[stride * other + index], strip)
            return strip
        beneath = jnp.zeros((1, LANES), jnp.float32)
        for other in range(faces - 1):
            beneath = beneath + jnp.where(level > other, rows[stride * other + index], 0.0)
        return strip + jnp.where(sub == 4, rolled(strip, -1, 0) * beneath, 0.0)

    def start(copy):
        copy.start()

    def wait_send(copy):
        copy.wait_send()

    for copy in taken[:2]:
        copy.wait()
    probe_h = per_probe(2)
    spread_h = per_panel(lambda f: spread_ref[2, 0, f])
    h = spread_h * probe_h
    column_f[...] = h
    rows_f[0] = h[0:1, :]
    rows_f[1] = h[SUBLANES - 1 : SUBLANES, :]
    low, high = columns_of((h,))
    rows_f[2] = low[0:1, :]
    rows_f[3] = high[0:1, :]
    pl.semaphore_wait(barrier, expected)
    for other in range(1, faces):
        @pl.when(level < other)
        def _():
            each_send(forward_rows, start, other)
            below_copy(other, level).start()

    probe_z, probe_m, probe_t = per_probe(0), per_probe(1), per_probe(3)
    spread_z, spread_m, spread_t = [
        per_panel(lambda f, c=c: spread_ref[c, 0, f]) for c in (0, 1, 3)
    ]
    for copy in taken[2:5]:
        copy.wait()
    u, v = [per_panel(lambda f, c=c: wind_ref[c, 0, f]) for c in range(2)]
    mass = per_panel(lambda f: mass_ref[0, f])
    heat = per_panel(lambda f: heat_ref[0, f])
    z, m, t = spread_z * probe_z, spread_m * probe_m, spread_t * probe_t
    fx = u * h + mass * z
    fy = v * h + mass * m

    def ghost_across(slots, row_slots, edge, part, is_row, is_adjoint):
        strip = jnp.zeros((SUBLANES, LANES), jnp.float32)
        reverse = jnp.zeros((SUBLANES, LANES), jnp.int32)
        entries = [strip] * 4
        for f in range(panels):
            source = links_ref[f, edge, 0]
            flip = links_ref[f, edge, 2]
            slot = links_ref[f, edge, 1] * 2 + jnp.where(flip == 1, 1 - part, part)
            held = with_levels(slots[slot], row_slots, 8, slot, is_adjoint)
            shift = (SUBLANES * (f - source) + LANES) % LANES
            here = panel_of == f
            strip = jnp.where(here, pltpu.roll(held, shift, 1), strip)
            reverse = jnp.where(here, flip, reverse)
            entries = [
                jnp.where(here, links_ref[f, edge, 3 + i].astype(jnp.float32), entries[i])
                for i in range(4)
            ]
        strip = jnp.where(reverse == 1, block_reversed(strip, inner), strip)
        m0, m1, m2, m3 = entries
        normal = m0 + m1 if is_row else m2 + m3
        first = m0 * strip + m1 * rolled(strip, -1, 0)
        second = m3 * strip + m2 * rolled(strip, 1, 0)
        if is_adjoint:
            vectors = jnp.where(sub == 0, first, second) * normal
            return jnp.where(
                sub < 2, vectors, jnp.where(sub == 3, strip, normal * strip)
            )
        vectors = jnp.where(sub == 0, first, second)
        return jnp.where(sub < 2, vectors, jnp.where(sub == 2, normal * strip, strip))

    def make_ghosts(buffers, rows_buffers, is_adjoint):
        strips, halo, slots = buffers[:3]
        row_halo, row_slots = rows_buffers[1:3]
        for d in range(4):
            @pl.when(~at[d])
            def _():
                ghosts[d] = with_levels(halo[d], row_halo, 4, d, is_adjoint)

        @pl.when(on_row)
        def _():
            ghosts[row_edge] = ghost_across(
                slots, row_slots, row_edge, row_part, True, is_adjoint
            )

        @pl.when(on_column)
        def _():
            ghosts[column_edge] = ghost_across(
                slots, row_slots, column_edge, column_part, False, is_adjoint
            )

    def slopes_of(x_fields, y_fields):
        low, high = ghosts[0], ghosts[1]
        east = []
        for c, field in enumerate(x_fields):
            before = jnp.where(sub == 0, low[c : c + 1, :], rolled(field, 1, 0))
            after = jnp.where(sub == SUBLANES - 1, high[c : c + 1, :], rolled(field, -1, 0))
            east.append(0.5 * (after - before))
        low = block_transposed(ghosts[2], sub, inner)
        high = block_transposed(ghosts[3], sub, inner)
        north = []
        for c, field in enumerate(y_fields):
            before = jnp.where(inner == 0, rolled(low, -c, 1), rolled(field, 1, 1))
            after = jnp.where(
                inner == SUBLANES - 1, rolled(high, SUBLANES - 1 - c, 1), rolled(field, -1, 1)
            )
            north.append(0.5 * (after - before))
        return east, north

    geo = t + heat * h
    write_strips(strips_f, (z, m, fx, t, geo, heat), (z, m, fy, t, geo, heat))
    each_send(forward, start)
    keep_own(strips_f, slots_f)
    for copy in taken[5:]:
        copy.wait()
    var_z, var_m, var_h, var_t = [
        per_panel(lambda f, c=c: variance_ref[c, 0, f]) for c in range(4)
    ]
    each_arrival(forward)
    for other in range(faces - 1):
        @pl.when(level > other)
        def _():
            below_copy(other, other).wait_recv()
            each_arrival(forward_rows, other)

    for other in range(faces - 1):
        geo = geo + heat * jnp.where(level > other, below_ref[other], 0.0)
    make_ghosts(forward, forward_rows, False)
    east, north = slopes_of((z, m, fx, t, geo), (z, m, fy, t, geo))
    zc = var_z * (z - time_increment * (east[4] + u * east[0] + v * north[0]))
    mc = var_m * (m - time_increment * (north[4] + u * east[1] + v * north[1]))
    hc = var_h * (h - time_increment * (east[2] + north[2]))
    tc = var_t * (t - time_increment * (u * east[3] + v * north[3]))

    x_fields, y_fields = (u * zc, u * mc, zc, hc, u * tc), (v * zc, v * mc, mc, hc, v * tc)
    write_strips(strips_a, x_fields, y_fields)
    for d in range(4):
        rows_a[d] = strips_a[d][2:3, :]
    column_a[0], column_a[1], column_a[2] = zc, mc, heat
    for other in range(faces):
        @pl.when(level > other)
        def _():
            each_send(adjoint_rows, start, other)

    each_send(adjoint, start)
    for other in range(faces):
        @pl.when(level > other)
        def _():
            above_copy(other, level).start()

    keep_own(strips_a, slots_a)
    each_arrival(adjoint)
    for other in range(1, faces):
        @pl.when(level < other)
        def _():
            above_copy(other, other).wait_recv()
            each_arrival(adjoint_rows, other)

    make_ghosts(adjoint, adjoint_rows, True)
    above = [above_ref[other] for other in range(1, faces)]
    east, north = slopes_of(
        x_fields + tuple(tiles[0] for tiles in above),
        y_fields + tuple(tiles[1] for tiles in above),
    )
    geo_back = time_increment * (east[2] + north[2])
    load = heat * geo_back
    for other, tiles in enumerate(above, 1):
        upper = tiles[2] * (time_increment * (east[4 + other] + north[4 + other]))
        load = load + jnp.where(level < other, upper, 0.0)

    flux_east = time_increment * east[3]
    flux_north = time_increment * north[3]
    z_back = zc + time_increment * (east[0] + north[0]) + mass * flux_east
    m_back = mc + time_increment * (east[1] + north[1]) + mass * flux_north
    t_back = tc + time_increment * (east[4] + north[4]) + geo_back
    h_back = hc + u * flux_east + v * flux_north + load
    out_ref[0] = probe_z + spread_z * z_back
    out_ref[1] = probe_m + spread_m * m_back
    out_ref[2] = probe_h + spread_h * h_back
    out_ref[3] = probe_t + spread_t * t_back

    each_send(forward, wait_send)
    each_send(adjoint, wait_send)
    for other in range(faces):
        @pl.when(level < other)
        def _():
            each_send(forward_rows, wait_send, other)
            below_copy(other, level).wait_send()

        @pl.when(level > other)
        def _():
            each_send(adjoint_rows, wait_send, other)
            above_copy(other, level).wait_send()


def unpack_kernel(packed_ref, out_ref):
    probe_count, components, _, panels, _, _ = out_ref.shape
    for component in range(components):
        tile = packed_ref[component]
        for p in range(probe_count):
            for f in range(panels):
                start = (p * panels + f) * SUBLANES
                out_ref[p, component, 0, f] = tile[:, start : start + SUBLANES]


def fused(count, faces, *operands):
    tile = (SUBLANES, LANES)
    vmem = pl.BlockSpec(memory_space=pltpu.VMEM)
    whole = pl.BlockSpec(memory_space=pl.ANY)
    probes = operands[0]
    strips = pltpu.VMEM((4, *tile), jnp.float32)
    slots = pltpu.VMEM((8, *tile), jnp.float32)

    def edge_rows(number):
        return pltpu.VMEM((number, 1, LANES), jnp.float32)

    dma = pltpu.SemaphoreType.DMA
    packed = pl.pallas_call(
        functools.partial(tile_kernel, count, faces),
        out_shape=pltpu.VMEM((probes.shape[1], *tile), probes.dtype),
        in_specs=[whole] * len(operands),
        out_specs=vmem,
        scratch_shapes=[pltpu.VMEM(x.shape, x.dtype) for x in operands[:-1]]
        + [
            pltpu.SMEM(operands[-1].shape, operands[-1].dtype),
            dma((len(operands),)),
        ]
        + [strips] * 4
        + [slots] * 2
        + [strips]
        + [pltpu.VMEM((faces, *tile), jnp.float32), pltpu.VMEM((faces, 3, *tile), jnp.float32)]
        + [pltpu.VMEM(tile, jnp.float32), pltpu.VMEM((3, *tile), jnp.float32)]
        + [edge_rows(4)] * 2
        + [edge_rows(4 * faces)] * 2
        + [edge_rows(8 * faces)] * 2
        + [dma((12,))] * 2
        + [dma((4,))] * 2
        + [dma((8,))] * 2
        + [dma((12 * faces,))] * 2
        + [dma((4 * faces,))] * 2
        + [dma((8 * faces,))] * 2
        + [dma((faces,))] * 4,
        compiler_params=pltpu.CompilerParams(collective_id=0, has_side_effects=True),
    )(*operands)
    return pl.pallas_call(
        unpack_kernel,
        out_shape=jax.ShapeDtypeStruct(probes.shape, probes.dtype),
        in_specs=[vmem],
        out_specs=vmem,
        compiler_params=pltpu.CompilerParams(vmem_limit_bytes=VMEM_BYTES),
    )(packed)


def solution(mesh):
    count, faces = mesh.shape["tx"], mesh.shape["face"]

    def chosen(*operands):
        probe_count, _, levels, panels, rows, columns = operands[0].shape
        fits = (
            levels == 1
            and count == mesh.shape["ty"]
            and count % 2 == 0
            and rows == columns == SUBLANES
            and faces + 4 <= SUBLANES
            and probe_count * panels * SUBLANES < LANES
        )
        return fused(count, faces, *operands) if fits else body(*operands)

    return jax.shard_map(
        chosen,
        mesh=mesh,
        in_specs=(
            P(None, None, "face", None, "tx", "ty"),
            P(None, "face", None, "tx", "ty"),
            P("face", None, "tx", "ty"),
            P("face", None, "tx", "ty"),
            P(None, "face", None, "tx", "ty"),
            P(None, "face", None, "tx", "ty"),
            P(),
        ),
        out_specs=P(None, None, "face", None, "tx", "ty"),
        check_vma=False,
    )
```

```python
import functools

import jax
import jax.numpy as jnp
from jax import lax
from jax.experimental import pallas as pl
from jax.experimental.pallas import tpu as pltpu
from jax.sharding import PartitionSpec as P

MESH = pl.DeviceIdType.MESH
SUBLANES = 8
LANES = 128
VMEM_BYTES = 4 * 2**20

time_increment = 0.3
forward_layout = (("vector", 0), ("vector", 2), ("scalar", 4), ("scalar", 5))
adjoint_layout = (("tensor", 0), ("vector", 4), ("scalar", 6), ("vector", 7))


def padded_2(array, sides, width):
    for axis, dim in sides:
        devices, length = (lax.axis_size(axis), array.shape[dim])
        up = [(i, (i + 1) % devices) for i in range(devices - 1)]
        down = [(j, i) for i, j in up]
        last = lax.slice_in_dim(array, length - width, length, axis=dim)
        leading = lax.slice_in_dim(array, 0, width, axis=dim)
        before = lax.ppermute(last, axis, up)
        after = lax.ppermute(leading, axis, down)
        array = jnp.concatenate([before, array, after], axis=dim)
    return array


def carried_in(value, axis, join, neutral, backward):
    count, mine = (lax.axis_size(axis), lax.axis_index(axis))
    pieces = lax.all_gather(value, axis)
    if backward:
        pieces = pieces[::-1]
        mine = count - 1 - mine
    total = jnp.full_like(value, 0) + jnp.asarray(neutral, value.dtype)

    def hop(position, total):
        longer = join(total, pieces[position])
        return jnp.where(position < mine, longer, total)

    return lax.fori_loop(0, count - 1, hop, total)


def carry_pair(leading, trailing, entries):
    return (
        entries[0] * leading + entries[1] * trailing,
        entries[2] * leading + entries[3] * trailing,
    )


def rotate_edge(edge_strip, matrix_codes, layout):
    matrix = matrix_codes.astype(edge_strip.dtype)
    entries = [matrix[:, column].reshape(1, 1, 6, 1) for column in range(4)]
    channels = [edge_strip[number] for number in range(edge_strip.shape[0])]
    for species, offset in layout:
        if species == "vector":
            channels[offset], channels[offset + 1] = carry_pair(
                channels[offset], channels[offset + 1], entries
            )
        elif species == "tensor":
            channels[offset], channels[offset + 1] = carry_pair(
                channels[offset], channels[offset + 1], entries
            )
            channels[offset + 2], channels[offset + 3] = carry_pair(
                channels[offset + 2], channels[offset + 3], entries
            )
            channels[offset], channels[offset + 2] = carry_pair(
                channels[offset], channels[offset + 2], entries
            )
            channels[offset + 1], channels[offset + 3] = carry_pair(
                channels[offset + 1], channels[offset + 3], entries
            )
    return jnp.stack(channels)


def orient(edge_rows, face_links, side, layout):
    source_face = face_links[:, side, 0]
    source_edge = face_links[:, side, 1]
    chosen = edge_rows[:, :, :, source_face, source_edge, :]
    flipped = (face_links[:, side, 2] == 1).reshape(1, 1, 1, 6, 1)
    chosen = jnp.where(flipped, chosen[..., ::-1], chosen)
    return rotate_edge(chosen, face_links[:, side, 3:7], layout)


def face_rows(fields):
    tile_row = lax.axis_index("tx")
    tile_column = lax.axis_index("ty")
    low_rows = jnp.where(tile_row == 0, fields[..., 0, :], 0.0)
    high_rows = jnp.where(tile_row == lax.axis_size("tx") - 1, fields[..., -1, :], 0.0)
    low_columns = jnp.where(tile_column == 0, fields[..., :, 0], 0.0)
    high_columns = jnp.where(tile_column == lax.axis_size("ty") - 1, fields[..., :, -1], 0.0)
    row_pair = jnp.stack([low_rows, high_rows], axis=4)
    column_pair = jnp.stack([low_columns, high_columns], axis=4)
    row_full = lax.psum(lax.all_gather(row_pair, "ty", axis=5, tiled=True), "tx")
    column_full = lax.psum(lax.all_gather(column_pair, "tx", axis=5, tiled=True), "ty")
    return jnp.concatenate([row_full, column_full], axis=4)


def extended_slopes(fields, face_links, layout):
    row_cells = fields.shape[4]
    column_cells = fields.shape[5]
    tile_row = lax.axis_index("tx")
    tile_column = lax.axis_index("ty")
    padded = padded_2(fields, (("tx", 4), ("ty", 5)), 1)
    edge_rows = face_rows(fields)
    western = lax.dynamic_slice_in_dim(
        orient(edge_rows, face_links, 0, layout), tile_column * column_cells, column_cells, 4
    )
    eastern = lax.dynamic_slice_in_dim(
        orient(edge_rows, face_links, 1, layout), tile_column * column_cells, column_cells, 4
    )
    southern = lax.dynamic_slice_in_dim(
        orient(edge_rows, face_links, 2, layout), tile_row * row_cells, row_cells, 4
    )
    northern = lax.dynamic_slice_in_dim(
        orient(edge_rows, face_links, 3, layout), tile_row * row_cells, row_cells, 4
    )
    row_number = lax.broadcasted_iota(jnp.int32, (row_cells, column_cells), 0)
    column_number = lax.broadcasted_iota(jnp.int32, (row_cells, column_cells), 1)
    first_row = (row_number == 0) & (tile_row == 0)
    last_row = (row_number == row_cells - 1) & (tile_row == lax.axis_size("tx") - 1)
    first_column = (column_number == 0) & (tile_column == 0)
    last_column = (column_number == column_cells - 1) & (tile_column == lax.axis_size("ty") - 1)
    east_slope_derivative = 0.5 * (padded[..., 2:, 1:-1] - padded[..., :-2, 1:-1])
    east_slope_derivative = (
        east_slope_derivative
        + jnp.where(last_row, 0.5 * eastern[..., None, :], 0.0)
        - jnp.where(first_row, 0.5 * western[..., None, :], 0.0)
    )
    north_slope_derivative = 0.5 * (padded[..., 1:-1, 2:] - padded[..., 1:-1, :-2])
    north_slope_derivative = (
        north_slope_derivative
        + jnp.where(last_column, 0.5 * northern[..., :, None], 0.0)
        - jnp.where(first_column, 0.5 * southern[..., :, None], 0.0)
    )
    return (east_slope_derivative, north_slope_derivative)


def pressure_of(sheet_depth_state):
    within = jnp.cumsum(sheet_depth_state, axis=1)
    totals_here = within[:, -1]
    underneath = carried_in(totals_here, "face", jnp.add, jnp.zeros_like(totals_here), False)
    return within + underneath[:, None]


def load_of(sensitivity):
    within = jnp.flip(jnp.cumsum(jnp.flip(sensitivity, 1), axis=1), 1)
    totals_here = within[:, 0]
    overhead = carried_in(totals_here, "face", jnp.add, jnp.zeros_like(totals_here), True)
    return within + overhead[:, None]


def body(
    probes,
    background_wind,
    layer_mass,
    trajectory_heat_factor,
    spread,
    inverse_misfit_variance,
    face_links,
):
    normalised_state_array = spread[None] * probes
    west_east_wind_part, south_north_wind_speed, sheet_depth_state, sheet_warmth_state = (
        normalised_state_array[:, 0],
        normalised_state_array[:, 1],
        normalised_state_array[:, 2],
        normalised_state_array[:, 3],
    )
    east_wind_speed, north_wind_speed = (background_wind[0], background_wind[1])
    ground_barometric_load = pressure_of(sheet_depth_state)
    gravity_potential_level = sheet_warmth_state + trajectory_heat_factor * ground_barometric_load
    east_mass_transport = east_wind_speed * sheet_depth_state + layer_mass * west_east_wind_part
    north_mass_transport = (
        north_wind_speed * sheet_depth_state + layer_mass * south_north_wind_speed
    )
    joined_state_arrays = jnp.stack(
        [
            west_east_wind_part,
            south_north_wind_speed,
            east_mass_transport,
            north_mass_transport,
            sheet_warmth_state,
            gravity_potential_level,
        ]
    )
    east_slope_derivative, north_slope_derivative = extended_slopes(
        joined_state_arrays, face_links, forward_layout
    )
    west_east_wind_after = west_east_wind_part - time_increment * (
        east_slope_derivative[5]
        + east_wind_speed * east_slope_derivative[0]
        + north_wind_speed * north_slope_derivative[0]
    )
    south_north_wind_after = south_north_wind_speed - time_increment * (
        north_slope_derivative[5]
        + east_wind_speed * east_slope_derivative[1]
        + north_wind_speed * north_slope_derivative[1]
    )
    depth_after_update = sheet_depth_state - time_increment * (
        east_slope_derivative[2] + north_slope_derivative[3]
    )
    warmth_after_update = sheet_warmth_state - time_increment * (
        east_wind_speed * east_slope_derivative[4] + north_wind_speed * north_slope_derivative[4]
    )
    zonal_cost = inverse_misfit_variance[0] * west_east_wind_after
    meridional_cost = inverse_misfit_variance[1] * south_north_wind_after
    thickness_cost = inverse_misfit_variance[2] * depth_after_update
    heat_misfit_penalty = inverse_misfit_variance[3] * warmth_after_update
    sensitive = jnp.stack(
        [
            east_wind_speed * zonal_cost,
            east_wind_speed * meridional_cost,
            north_wind_speed * zonal_cost,
            north_wind_speed * meridional_cost,
            zonal_cost,
            meridional_cost,
            thickness_cost,
            east_wind_speed * heat_misfit_penalty,
            north_wind_speed * heat_misfit_penalty,
        ]
    )
    east_slope_derivative, north_slope_derivative = extended_slopes(
        sensitive, face_links, adjoint_layout
    )
    geo_back = time_increment * (east_slope_derivative[4] + north_slope_derivative[5])
    flux_east_back = time_increment * east_slope_derivative[6]
    flux_north_back = time_increment * north_slope_derivative[6]
    zonal_back = (
        zonal_cost
        + time_increment * (east_slope_derivative[0] + north_slope_derivative[2])
        + layer_mass * flux_east_back
    )
    meridional_back = (
        meridional_cost
        + time_increment * (east_slope_derivative[1] + north_slope_derivative[3])
        + layer_mass * flux_north_back
    )
    warmth_back = (
        heat_misfit_penalty
        + time_increment * (east_slope_derivative[7] + north_slope_derivative[8])
        + geo_back
    )
    thickness_back = (
        thickness_cost
        + east_wind_speed * flux_east_back
        + north_wind_speed * flux_north_back
        + load_of(trajectory_heat_factor * geo_back)
    )
    adjoint_out = jnp.stack([zonal_back, meridional_back, thickness_back, warmth_back], axis=1)
    return probes + spread[None] * adjoint_out


def rolled(tile, shift, axis):
    return pltpu.roll(tile, shift % tile.shape[axis], axis)


def gathered(tile, index, axis):
    return jnp.take_along_axis(tile, index, axis=axis, mode="promise_in_bounds")


def block_transposed(tile, sub, inner):
    base = lax.broadcasted_iota(jnp.int32, tile.shape, 1) - inner
    skew = (inner - sub + SUBLANES) % SUBLANES
    tile = gathered(tile, base + skew, 1)
    tile = gathered(tile, skew, 0)
    return gathered(tile, base + (inner + sub) % SUBLANES, 1)


def block_reversed(tile, inner):
    lane = lax.broadcasted_iota(jnp.int32, tile.shape, 1)
    return gathered(tile, lane - inner + (SUBLANES - 1 - inner), 1)


def tile_kernel(
    count,
    faces,
    probes_hbm,
    wind_hbm,
    mass_hbm,
    heat_hbm,
    spread_hbm,
    variance_hbm,
    links_hbm,
    out_ref,
    probes_ref,
    wind_ref,
    mass_ref,
    heat_ref,
    spread_ref,
    variance_ref,
    links_ref,
    take_sem,
    strips_f,
    strips_a,
    halo_f,
    halo_a,
    slots_f,
    slots_a,
    ghosts,
    below_ref,
    above_ref,
    column_f,
    column_a,
    rows_f,
    rows_a,
    row_halo_f,
    row_halo_a,
    row_slots_f,
    row_slots_a,
    send_f,
    send_a,
    recv_halo_f,
    recv_halo_a,
    recv_slot_f,
    recv_slot_a,
    send_rows_f,
    send_rows_a,
    recv_row_halo_f,
    recv_row_halo_a,
    recv_row_slot_f,
    recv_row_slot_a,
    send_below,
    send_above,
    recv_below,
    recv_above,
):
    level = lax.axis_index("face")
    row = lax.axis_index("tx")
    column = lax.axis_index("ty")
    probe_count = probes_ref.shape[0]
    panels = probes_ref.shape[3]
    last = count - 1
    at = [row == 0, row == last, column == 0, column == last]
    on_row = at[0] | at[1]
    on_column = at[2] | at[3]
    corner = on_row & on_column
    middle = (on_row | on_column) & ~corner
    row_edge = jnp.where(at[0], 0, 1)
    column_edge = jnp.where(at[2], 2, 3)
    half = count // 2
    row_part = jnp.where(column < half, 0, 1)
    column_part = jnp.where(row < half, 0, 1)
    row_slot = row_edge * 2 + row_part
    column_slot = column_edge * 2 + column_part
    own_edge = jnp.where(on_row, row_edge, column_edge)
    own_slot = jnp.where(on_row, row_slot, column_slot)
    along = jnp.where(on_row, column, row)
    near = jnp.where(along < half, along, last - along)

    def slot_place(edge, part):
        segment = near if part == 0 else last - near
        return [(0, segment), (last, segment), (segment, 0), (segment, last)][edge]

    beside = [(row - 1, column), (row + 1, column), (row, column - 1), (row, column + 1)]
    corners = [(0, 0), (0, last), (last, 0), (last, last)]

    barrier = pltpu.get_barrier_semaphore()

    def greet(other, place):
        pl.semaphore_signal(
            barrier,
            inc=1,
            device_id={"face": other, "tx": place[0], "ty": place[1]},
            device_id_type=MESH,
        )

    for other in range(faces):
        for d in range(4):
            @pl.when(~at[d])
            def _():
                greet(other, beside[d])

        @pl.when(middle)
        def _():
            for slot in range(8):
                @pl.when((own_slot != slot) | (level != other))
                def _():
                    greet(other, slot_place(slot // 2, slot % 2))

        @pl.when(corner)
        def _():
            for place in corners:
                @pl.when((row != place[0]) | (column != place[1]) | (level != other))
                def _():
                    greet(other, place)

        @pl.when(level != other)
        def _():
            greet(other, (row, column))

    taken = [
        pltpu.make_async_copy(source, target, take_sem.at[i])
        for i, (source, target) in enumerate(
            (
                (probes_hbm, probes_ref),
                (spread_hbm, spread_ref),
                (wind_hbm, wind_ref),
                (mass_hbm, mass_ref),
                (heat_hbm, heat_ref),
                (variance_hbm, variance_ref),
                (links_hbm, links_ref),
            )
        )
    ]
    for copy in taken:
        copy.start()

    expected = (
        faces - 1 + jnp.where(middle, 8 * faces - 1, 0) + jnp.where(corner, 4 * faces - 1, 0)
    )
    for d in range(4):
        expected = expected + jnp.where(at[d], 0, faces)

    sub = lax.broadcasted_iota(jnp.int32, (SUBLANES, LANES), 0)
    lane = lax.broadcasted_iota(jnp.int32, (SUBLANES, LANES), 1)
    inner = lane % SUBLANES
    panel_of = (lane // SUBLANES) % panels

    def packed(tiles):
        width = LANES - SUBLANES * len(tiles)
        return jnp.concatenate(tiles + [jnp.zeros((SUBLANES, width), jnp.float32)], axis=1)

    def per_panel(load):
        return packed([load(f) for f in range(panels)] * probe_count)

    def per_probe(component):
        return packed(
            [
                probes_ref[p, component, 0, f]
                for p in range(probe_count)
                for f in range(panels)
            ]
        )

    def level_copy(other, source, target, send, recv):
        return pltpu.make_async_remote_copy(
            src_ref=source,
            dst_ref=target,
            send_sem=send,
            recv_sem=recv,
            device_id={"face": other},
            device_id_type=MESH,
        )

    def below_copy(other, slot):
        return level_copy(
            other, column_f, below_ref.at[slot], send_below.at[other], recv_below.at[slot]
        )

    def above_copy(other, slot):
        return level_copy(
            other, column_a, above_ref.at[slot], send_above.at[other], recv_above.at[slot]
        )

    nothing = jnp.zeros((SUBLANES, LANES), jnp.float32)

    def columns_of(y_fields):
        low = high = nothing
        for c, field in enumerate(y_fields):
            low = jnp.where(inner == c, rolled(field, c, 1), low)
            high = jnp.where(inner == c, rolled(field, c - (SUBLANES - 1), 1), high)
        return block_transposed(low, sub, inner), block_transposed(high, sub, inner)

    def write_strips(strips, x_fields, y_fields):
        low = high = nothing
        for c, field in enumerate(x_fields):
            low = jnp.where(sub == c, field[0:1, :], low)
            high = jnp.where(sub == c, field[SUBLANES - 1 : SUBLANES, :], high)
        strips[0] = low
        strips[1] = high
        strips[2], strips[3] = columns_of(y_fields)

    def strip_copy(source, target, send, recv, other, place):
        return pltpu.make_async_remote_copy(
            src_ref=source,
            dst_ref=target,
            send_sem=send,
            recv_sem=recv,
            device_id={"face": other, "tx": place[0], "ty": place[1]},
            device_id_type=MESH,
        )

    def each_send(buffers, act, target=None):
        strips, halo, slots, send, recv_halo, recv_slot = buffers
        across = target is not None
        other = target if across else level
        first_send = 12 * target if across else 0
        first_halo = 4 * level if across else 0
        first_slot = 8 * level if across else 0

        @pl.when(middle)
        def _():
            for slot in range(8):
                @pl.when((own_slot != slot) | across)
                def _():
                    act(
                        strip_copy(
                            strips.at[own_edge],
                            slots.at[first_slot + own_slot],
                            send.at[first_send + 4 + slot],
                            recv_slot.at[first_slot + own_slot],
                            other,
                            slot_place(slot // 2, slot % 2),
                        )
                    )

        @pl.when(corner)
        def _():
            for number, place in enumerate(corners):
                @pl.when((row != place[0]) | (column != place[1]) | across)
                def _():
                    for kind, (edge, slot) in enumerate(
                        ((row_edge, row_slot), (column_edge, column_slot))
                    ):
                        act(
                            strip_copy(
                                strips.at[edge],
                                slots.at[first_slot + slot],
                                send.at[first_send + 4 + number * 2 + kind],
                                recv_slot.at[first_slot + slot],
                                other,
                                place,
                            )
                        )

        for d in range(4):
            @pl.when(~at[d])
            def _():
                act(
                    strip_copy(
                        strips.at[d],
                        halo.at[first_halo + (d ^ 1)],
                        send.at[first_send + d],
                        recv_halo.at[first_halo + (d ^ 1)],
                        other,
                        beside[d],
                    )
                )

    def each_arrival(buffers, source=None):
        strips, halo, slots, send, recv_halo, recv_slot = buffers
        across = source is not None
        first_halo = 4 * source if across else 0
        first_slot = 8 * source if across else 0

        def arrival(target, semaphore):
            strip_copy(
                strips.at[0], target, send.at[0], semaphore, level, (row, column)
            ).wait_recv()

        for d in range(4):
            @pl.when(~at[d])
            def _():
                arrival(halo.at[first_halo + d], recv_halo.at[first_halo + d])

        @pl.when(on_row | on_column)
        def _():
            for slot in range(8):
                mine = (on_row & (row_slot == slot)) | (on_column & (column_slot == slot))

                @pl.when(~mine | across)
                def _():
                    arrival(slots.at[first_slot + slot], recv_slot.at[first_slot + slot])

    forward = (strips_f, halo_f, slots_f, send_f, recv_halo_f, recv_slot_f)
    adjoint = (strips_a, halo_a, slots_a, send_a, recv_halo_a, recv_slot_a)
    forward_rows = (
        rows_f, row_halo_f, row_slots_f, send_rows_f, recv_row_halo_f, recv_row_slot_f
    )
    adjoint_rows = (
        rows_a, row_halo_a, row_slots_a, send_rows_a, recv_row_halo_a, recv_row_slot_a
    )

    def keep_own(strips, slots):
        @pl.when(on_row)
        def _():
            slots[row_slot] = strips[row_edge]

        @pl.when(on_column)
        def _():
            slots[column_slot] = strips[column_edge]

    def with_levels(strip, rows, stride, index, is_adjoint):
        if is_adjoint:
            for other in range(1, faces):
                strip = jnp.where(sub == 4 + other, rows[stride * other + index], strip)
            return strip
        beneath = jnp.zeros((1, LANES), jnp.float32)
        for other in range(faces - 1):
            beneath = beneath + jnp.where(level > other, rows[stride * other + index], 0.0)
        return strip + jnp.where(sub == 4, rolled(strip, -1, 0) * beneath, 0.0)

    def start(copy):
        copy.start()

    def wait_send(copy):
        copy.wait_send()

    for copy in taken[:2]:
        copy.wait()
    probe_h = per_probe(2)
    spread_h = per_panel(lambda f: spread_ref[2, 0, f])
    h = spread_h * probe_h
    column_f[...] = h
    rows_f[0] = h[0:1, :]
    rows_f[1] = h[SUBLANES - 1 : SUBLANES, :]
    low, high = columns_of((h,))
    rows_f[2] = low[0:1, :]
    rows_f[3] = high[0:1, :]
    pl.semaphore_wait(barrier, expected)
    for other in range(1, faces):
        @pl.when(level < other)
        def _():
            each_send(forward_rows, start, other)
            below_copy(other, level).start()

    probe_z, probe_m, probe_t = per_probe(0), per_probe(1), per_probe(3)
    spread_z, spread_m, spread_t = [
        per_panel(lambda f, c=c: spread_ref[c, 0, f]) for c in (0, 1, 3)
    ]
    for copy in taken[2:5]:
        copy.wait()
    u, v = [per_panel(lambda f, c=c: wind_ref[c, 0, f]) for c in range(2)]
    mass = per_panel(lambda f: mass_ref[0, f])
    heat = per_panel(lambda f: heat_ref[0, f])
    z, m, t = spread_z * probe_z, spread_m * probe_m, spread_t * probe_t
    fx = u * h + mass * z
    fy = v * h + mass * m

    def ghost_across(slots, row_slots, edge, part, is_row, is_adjoint):
        strip = jnp.zeros((SUBLANES, LANES), jnp.float32)
        reverse = jnp.zeros((SUBLANES, LANES), jnp.int32)
        entries = [strip] * 4
        for f in range(panels):
            source = links_ref[f, edge, 0]
            flip = links_ref[f, edge, 2]
            slot = links_ref[f, edge, 1] * 2 + jnp.where(flip == 1, 1 - part, part)
            held = with_levels(slots[slot], row_slots, 8, slot, is_adjoint)
            shift = (SUBLANES * (f - source) + LANES) % LANES
            here = panel_of == f
            strip = jnp.where(here, pltpu.roll(held, shift, 1), strip)
            reverse = jnp.where(here, flip, reverse)
            entries = [
                jnp.where(here, links_ref[f, edge, 3 + i].astype(jnp.float32), entries[i])
                for i in range(4)
            ]
        strip = jnp.where(reverse == 1, block_reversed(strip, inner), strip)
        m0, m1, m2, m3 = entries
        normal = m0 + m1 if is_row else m2 + m3
        first = m0 * strip + m1 * rolled(strip, -1, 0)
        second = m3 * strip + m2 * rolled(strip, 1, 0)
        if is_adjoint:
            vectors = jnp.where(sub == 0, first, second) * normal
            return jnp.where(
                sub < 2, vectors, jnp.where(sub == 3, strip, normal * strip)
            )
        vectors = jnp.where(sub == 0, first, second)
        return jnp.where(sub < 2, vectors, jnp.where(sub == 2, normal * strip, strip))

    def make_ghosts(buffers, rows_buffers, is_adjoint):
        strips, halo, slots = buffers[:3]
        row_halo, row_slots = rows_buffers[1:3]
        for d in range(4):
            @pl.when(~at[d])
            def _():
                ghosts[d] = with_levels(halo[d], row_halo, 4, d, is_adjoint)

        @pl.when(on_row)
        def _():
            ghosts[row_edge] = ghost_across(
                slots, row_slots, row_edge, row_part, True, is_adjoint
            )

        @pl.when(on_column)
        def _():
            ghosts[column_edge] = ghost_across(
                slots, row_slots, column_edge, column_part, False, is_adjoint
            )

    def slopes_of(x_fields, y_fields):
        low, high = ghosts[0], ghosts[1]
        east = []
        for c, field in enumerate(x_fields):
            before = jnp.where(sub == 0, low[c : c + 1, :], rolled(field, 1, 0))
            after = jnp.where(sub == SUBLANES - 1, high[c : c + 1, :], rolled(field, -1, 0))
            east.append(0.5 * (after - before))
        low = block_transposed(ghosts[2], sub, inner)
        high = block_transposed(ghosts[3], sub, inner)
        north = []
        for c, field in enumerate(y_fields):
            before = jnp.where(inner == 0, rolled(low, -c, 1), rolled(field, 1, 1))
            after = jnp.where(
                inner == SUBLANES - 1, rolled(high, SUBLANES - 1 - c, 1), rolled(field, -1, 1)
            )
            north.append(0.5 * (after - before))
        return east, north

    geo = t + heat * h
    write_strips(strips_f, (z, m, fx, t, geo, heat), (z, m, fy, t, geo, heat))
    each_send(forward, start)
    keep_own(strips_f, slots_f)
    for copy in taken[5:]:
        copy.wait()
    var_z, var_m, var_h, var_t = [
        per_panel(lambda f, c=c: variance_ref[c, 0, f]) for c in range(4)
    ]
    each_arrival(forward)
    for other in range(faces - 1):
        @pl.when(level > other)
        def _():
            below_copy(other, other).wait_recv()
            each_arrival(forward_rows, other)

    for other in range(faces - 1):
        geo = geo + heat * jnp.where(level > other, below_ref[other], 0.0)
    make_ghosts(forward, forward_rows, False)
    east, north = slopes_of((z, m, fx, t, geo), (z, m, fy, t, geo))
    zc = var_z * (z - time_increment * (east[4] + u * east[0] + v * north[0]))
    mc = var_m * (m - time_increment * (north[4] + u * east[1] + v * north[1]))
    hc = var_h * (h - time_increment * (east[2] + north[2]))
    tc = var_t * (t - time_increment * (u * east[3] + v * north[3]))

    x_fields, y_fields = (u * zc, u * mc, zc, hc, u * tc), (v * zc, v * mc, mc, hc, v * tc)
    write_strips(strips_a, x_fields, y_fields)
    for d in range(4):
        rows_a[d] = strips_a[d][2:3, :]
    column_a[0], column_a[1], column_a[2] = zc, mc, heat
    for other in range(faces):
        @pl.when(level > other)
        def _():
            each_send(adjoint_rows, start, other)

    each_send(adjoint, start)
    for other in range(faces):
        @pl.when(level > other)
        def _():
            above_copy(other, level).start()

    keep_own(strips_a, slots_a)
    each_arrival(adjoint)
    for other in range(1, faces):
        @pl.when(level < other)
        def _():
            above_copy(other, other).wait_recv()
            each_arrival(adjoint_rows, other)

    make_ghosts(adjoint, adjoint_rows, True)
    above = [above_ref[other] for other in range(1, faces)]
    east, north = slopes_of(
        x_fields + tuple(tiles[0] for tiles in above),
        y_fields + tuple(tiles[1] for tiles in above),
    )
    geo_back = time_increment * (east[2] + north[2])
    load = heat * geo_back
    for other, tiles in enumerate(above, 1):
        upper = tiles[2] * (time_increment * (east[4 + other] + north[4 + other]))
        load = load + jnp.where(level < other, upper, 0.0)

    flux_east = time_increment * east[3]
    flux_north = time_increment * north[3]
    z_back = zc + time_increment * (east[0] + north[0]) + mass * flux_east
    m_back = mc + time_increment * (east[1] + north[1]) + mass * flux_north
    t_back = tc + time_increment * (east[4] + north[4]) + geo_back
    h_back = hc + u * flux_east + v * flux_north + load
    out_ref[0] = probe_z + spread_z * z_back
    out_ref[1] = probe_m + spread_m * m_back
    out_ref[2] = probe_h + spread_h * h_back
    out_ref[3] = probe_t + spread_t * t_back

    each_send(forward, wait_send)
    each_send(adjoint, wait_send)
    for other in range(faces):
        @pl.when(level < other)
        def _():
            each_send(forward_rows, wait_send, other)
            below_copy(other, level).wait_send()

        @pl.when(level > other)
        def _():
            each_send(adjoint_rows, wait_send, other)
            above_copy(other, level).wait_send()


def unpack_kernel(packed_ref, out_ref):
    probe_count, components, _, panels, _, _ = out_ref.shape
    for component in range(components):
        tile = packed_ref[component]
        for p in range(probe_count):
            for f in range(panels):
                start = (p * panels + f) * SUBLANES
                out_ref[p, component, 0, f] = tile[:, start : start + SUBLANES]


def fused(count, faces, *operands):
    tile = (SUBLANES, LANES)
    vmem = pl.BlockSpec(memory_space=pltpu.VMEM)
    whole = pl.BlockSpec(memory_space=pl.ANY)
    probes = operands[0]
    strips = pltpu.VMEM((4, *tile), jnp.float32)
    slots = pltpu.VMEM((8, *tile), jnp.float32)

    def edge_rows(number):
        return pltpu.VMEM((number, 1, LANES), jnp.float32)

    dma = pltpu.SemaphoreType.DMA
    packed = pl.pallas_call(
        functools.partial(tile_kernel, count, faces),
        out_shape=pltpu.VMEM((probes.shape[1], *tile), probes.dtype),
        in_specs=[whole] * len(operands),
        out_specs=vmem,
        scratch_shapes=[pltpu.VMEM(x.shape, x.dtype) for x in operands[:-1]]
        + [
            pltpu.SMEM(operands[-1].shape, operands[-1].dtype),
            dma((len(operands),)),
        ]
        + [strips] * 4
        + [slots] * 2
        + [strips]
        + [pltpu.VMEM((faces, *tile), jnp.float32), pltpu.VMEM((faces, 3, *tile), jnp.float32)]
        + [pltpu.VMEM(tile, jnp.float32), pltpu.VMEM((3, *tile), jnp.float32)]
        + [edge_rows(4)] * 2
        + [edge_rows(4 * faces)] * 2
        + [edge_rows(8 * faces)] * 2
        + [dma((12,))] * 2
        + [dma((4,))] * 2
        + [dma((8,))] * 2
        + [dma((12 * faces,))] * 2
        + [dma((4 * faces,))] * 2
        + [dma((8 * faces,))] * 2
        + [dma((faces,))] * 4,
        compiler_params=pltpu.CompilerParams(collective_id=0, has_side_effects=True),
    )(*operands)
    return pl.pallas_call(
        unpack_kernel,
        out_shape=jax.ShapeDtypeStruct(probes.shape, probes.dtype),
        in_specs=[vmem],
        out_specs=vmem,
        compiler_params=pltpu.CompilerParams(vmem_limit_bytes=VMEM_BYTES),
    )(packed)


def solution(mesh):
    count, faces = mesh.shape["tx"], mesh.shape["face"]

    def chosen(*operands):
        probe_count, _, levels, panels, rows, columns = operands[0].shape
        fits = (
            levels == 1
            and count == mesh.shape["ty"]
            and count % 2 == 0
            and rows == columns == SUBLANES
            and faces + 4 <= SUBLANES
            and probe_count * panels * SUBLANES < LANES
        )
        return fused(count, faces, *operands) if fits else body(*operands)

    return jax.shard_map(
        chosen,
        mesh=mesh,
        in_specs=(
            P(None, None, "face", None, "tx", "ty"),
            P(None, "face", None, "tx", "ty"),
            P("face", None, "tx", "ty"),
            P("face", None, "tx", "ty"),
            P(None, "face", None, "tx", "ty"),
            P(None, "face", None, "tx", "ty"),
            P(),
        ),
        out_specs=P(None, None, "face", None, "tx", "ty"),
        check_vma=False,
    )
```
